32 devices in a mesh: gx: 8 (over z, y), gy: 4 (over x, core).
Axes of the slice: x: 2, y: 2, z: 4, core: 2. Of those that a mesh axis runs over, the one named last changes fastest.
Arguments:
- scalars: float32 [20, 64, 64, 128], P(None, 'gx', 'gy'), may hold values from -6 to 6
- velocity: float32 [3, 64, 64, 128], P(None, 'gx', 'gy'), may hold values from -4 to 4
- diffusivity: float32 [64, 64, 128], P('gx', 'gy'), may hold values from 0.05 to 0.6
- burn_list: int32 [8, 4, 64], P('gx', 'gy'), may hold values from 0 to 128, as said below
- w_in: bfloat16 [800, 20], replicated, may hold values from -1.25 to 1.25
- w_mid: bfloat16 [400, 800], replicated, may hold values from -0.21875 to 0.21875
- w_out: bfloat16 [20, 400], replicated, may hold values from -0.3125 to 0.3125
Outputs:
- scalars_out: float32 [20, 64, 64, 128], P(None, 'gx', 'gy')
- velocity_out: float32 [3, 64, 64, 128], P(None, 'gx', 'gy')
The draws below stay inside these ranges and needn't reach their ends.
Inputs may be any that keep to these rules, and one draw needn't show every extreme that they name: `burn_list`: in each device's list the burning columns come first, distinct, and the remaining slots hold 128. A device lists 0 to 64 burning columns; in every group of devices with one gx index one device lists 64 and one lists none, and the group lists exactly 128 together.
All inputs are finite; a program needn't handle non-finite values.
Results may differ from the reference program's by a relative error of at most 0.0023.
Values may be sent and summed in bfloat16 or wider, within the bound.
A program may use at most 64 MiB of HBM per device.

```python
import math
import jax
import jax.numpy as jnp
from jax import lax

CX = 8
CY = 16
NZ = 128
NS = 20
H1 = 800
H2 = 400
NX = 64
NY = 64
NB = 128
BURN_DEV = 32
MAXB = 64
N_GX = 8
N_GY = 4


def draw_burn_list(key, part):
    first_key, second_key, third_key = jax.random.split(jax.random.fold_in(key, 7), 3)
    half_group = N_GY // 2
    amount = jax.random.randint(first_key, (N_GX, half_group), 0, BURN_DEV + 1).astype(jnp.int32)
    amount = amount.at[:, 0].set(BURN_DEV)
    counts = jnp.concatenate([BURN_DEV + amount, BURN_DEV - amount], axis=1)
    scores = jax.random.randint(second_key, (N_GX, N_GY), 0, 1 << 20).astype(jnp.int32) * N_GY + jnp.arange(N_GY, dtype=jnp.int32)[None, :]
    shuffle = jnp.argsort(scores, axis=1)
    counts = jnp.take_along_axis(counts, shuffle, axis=1)
    col_scores = jax.random.randint(third_key, (N_GX, N_GY, NB), 0, 1 << 16).astype(jnp.int32) * NB + jnp.arange(NB, dtype=jnp.int32)[None, None, :]
    columns = jnp.argsort(col_scores, axis=2)[:, :, :MAXB].astype(jnp.int32)
    active = jnp.arange(MAXB, dtype=jnp.int32)[None, None, :] < counts[:, :, None]
    return jnp.where(active, columns, NB).astype(jnp.int32)


def levels(key, extent, cuts, smallest, top_value):
    def one(axis_at, shards_of):
        steps = jax.random.uniform(jax.random.fold_in(jax.random.fold_in(key, 6), axis_at), (shards_of,), jnp.float32, smallest / len(cuts), top_value / len(cuts))
        return jnp.repeat(jnp.exp(steps), extent[axis_at] // shards_of).reshape((-1,) + (1,) * (len(extent) - axis_at - 1))

    level = one(*cuts[0])
    for cut in cuts[1:]:
        level = level * one(*cut)
    return level


def centred(own_key, dims, scale, limit, cuts=(), kind=jnp.bfloat16):
    array = scale * jax.random.normal(own_key, dims, jnp.float32)
    if cuts:
        array = array * levels(own_key, dims, cuts, -0.22, 0.18)
    return jnp.clip(array, -limit, limit).astype(kind)


def setup_inputs(seed: int = 0) -> dict:
    seeds = jax.random.split(jax.random.key(seed), 8)
    scalars = centred(seeds[0], (NS, NX, NY, NZ), 1.0, 6.0, ((1, 8), (2, 4)), jnp.float32)
    velocity = centred(seeds[1], (3, NX, NY, NZ), 1.0, 4.0, ((1, 8), (2, 4)), jnp.float32)
    diffusivity = jnp.clip(jnp.exp(math.log(0.6) - 2.4849067 * jax.random.uniform(seeds[2], (NX, NY, NZ), jnp.float32) ** levels(seeds[2], (NX, NY, NZ), ((0, 8), (1, 4)), -0.2, 0.2)), 0.05, 0.6)
    burn_list = draw_burn_list(jax.random.fold_in(seeds[7], 71), 0)
    w_in = centred(seeds[4], (H1, NS), NS ** -0.5, 1.25)
    w_mid = centred(seeds[5], (H2, H1), H1 ** -0.5, 0.21875)
    w_out = centred(seeds[6], (NS, H2), H2 ** -0.5, 0.3125)
    return {"scalars": scalars, "velocity": velocity, "diffusivity": diffusivity, "burn_list": burn_list, "w_in": w_in, "w_mid": w_mid, "w_out": w_out}


time_step = 0.25

def hartley_table(length):
    position = jnp.arange(length, dtype=jnp.int32)
    product = position[:, None] * position[None, :] % length
    phase_angle = 2.0 * math.pi / length * product.astype(jnp.float32)
    return (jnp.cos(phase_angle) + jnp.sin(phase_angle)) / math.sqrt(length)

def cosine_table(length):
    position = jnp.arange(length, dtype=jnp.int32)
    product = position[:, None] * (2 * position[None, :] + 1) % (4 * length)
    phase_angle = math.pi / (2 * length) * product.astype(jnp.float32)
    weight = jnp.where(position == 0, math.sqrt(1.0 / length), math.sqrt(2.0 / length)).astype(jnp.float32)
    return weight[:, None] * jnp.cos(phase_angle)

def depth_next(values):
    return jnp.concatenate([values[..., 1:], values[..., -1:]], -1)

def depth_prev(values):
    return jnp.concatenate([values[..., :1], values[..., :-1]], -1)

def transport_rate(values, velocity, diffusivity):
    x_next = jnp.roll(values, -1, 0)
    x_prev = jnp.roll(values, 1, 0)
    y_next = jnp.roll(values, -1, 1)
    y_prev = jnp.roll(values, 1, 1)
    z_next = depth_next(values)
    z_prev = depth_prev(values)
    coefficient = diffusivity
    advection = velocity[0] * (x_next - x_prev) * 0.5 + velocity[1] * (y_next - y_prev) * 0.5 + velocity[2] * (z_next - z_prev) * 0.5
    diffusion = 0.5 * (coefficient + jnp.roll(coefficient, -1, 0)) * (x_next - values) - 0.5 * (coefficient + jnp.roll(coefficient, 1, 0)) * (values - x_prev)
    diffusion = diffusion + 0.5 * (coefficient + jnp.roll(coefficient, -1, 1)) * (y_next - values) - 0.5 * (coefficient + jnp.roll(coefficient, 1, 1)) * (values - y_prev)
    diffusion = diffusion + 0.5 * (coefficient + depth_next(coefficient)) * (z_next - values) - 0.5 * (coefficient + depth_prev(coefficient)) * (values - z_prev)
    return diffusion - advection

def network(blocks, w_in, w_mid, w_out):
    hidden_one = jnp.einsum('hn,bnz->bhz', w_in.astype(jnp.float32), blocks.astype(jnp.float32))
    hidden_one = jax.nn.gelu(hidden_one).astype(jnp.bfloat16)
    hidden_two = jnp.einsum('kh,bhz->bkz', w_mid.astype(jnp.float32), hidden_one.astype(jnp.float32))
    hidden_two = jax.nn.gelu(hidden_two).astype(jnp.bfloat16)
    return jnp.einsum('nk,bkz->bnz', w_out.astype(jnp.float32), hidden_two.astype(jnp.float32))

def reference(scalars, velocity, diffusivity, burn_list, w_in, w_mid, w_out):

    def advance(values):
        section_one = values + time_step * transport_rate(values, velocity, diffusivity)
        return 0.5 * values + 0.5 * (section_one + time_step * transport_rate(section_one, velocity, diffusivity))
    transported = lax.map(advance, scalars)
    blocked = transported.reshape(NS, N_GX, CX, N_GY, CY, NZ).transpose(1, 3, 0, 2, 4, 5).reshape(N_GX * N_GY, NS, CX * CY, NZ)
    listing = burn_list.reshape(N_GX * N_GY, MAXB)

    def react(member):
        values, listed = member
        picked = jnp.take(values, jnp.minimum(listed, CX * CY - 1), axis=1)
        feed = jnp.transpose(picked, (1, 0, 2)).astype(jnp.bfloat16)
        reaction = network(feed, w_in, w_mid, w_out)
        return values.at[:, listed].add(jnp.transpose(reaction, (1, 0, 2)), mode='drop')
    burned = lax.map(react, (blocked, listing))
    scalars_out = burned.reshape(N_GX, N_GY, NS, CX, CY, NZ).transpose(2, 0, 3, 1, 4, 5).reshape(NS, NX, NY, NZ)
    divergence = 0.5 * (jnp.roll(velocity[0], -1, 0) - jnp.roll(velocity[0], 1, 0))
    divergence = divergence + 0.5 * (jnp.roll(velocity[1], -1, 1) - jnp.roll(velocity[1], 1, 1))
    divergence = divergence + 0.5 * (depth_next(velocity[2]) - depth_prev(velocity[2]))
    highest = lax.Precision.HIGHEST
    table_x = hartley_table(NX)
    table_y = hartley_table(NY)
    table_z = cosine_table(NZ)
    spectrum = jnp.einsum('az,xyz->xya', table_z, divergence, precision=highest)
    spectrum = jnp.einsum('by,xyz->xbz', table_y, spectrum, precision=highest)
    spectrum = jnp.einsum('cx,xyz->cyz', table_x, spectrum, precision=highest)
    mode_x = jnp.arange(NX, dtype=jnp.int32)
    mode_y = jnp.arange(NY, dtype=jnp.int32)
    mode_z = jnp.arange(NZ, dtype=jnp.int32)
    eigen_x = 2.0 - 2.0 * jnp.cos(2.0 * math.pi / NX * mode_x.astype(jnp.float32))
    eigen_y = 2.0 - 2.0 * jnp.cos(2.0 * math.pi / NY * mode_y.astype(jnp.float32))
    eigen_z = 2.0 - 2.0 * jnp.cos(math.pi / NZ * mode_z.astype(jnp.float32))
    eigen = eigen_x[:, None, None] + eigen_y[None, :, None] + eigen_z[None, None, :]
    anchor = ((mode_x[:, None, None] == 0) & (mode_y[None, :, None] == 0) & (mode_z[None, None, :] == 0)).astype(jnp.float32)
    solved = -spectrum * (1.0 - anchor) / (eigen + anchor)
    solved = jnp.einsum('cx,xyz->cyz', table_x, solved, precision=highest)
    solved = jnp.einsum('by,xyz->xbz', table_y, solved, precision=highest)
    pressure = jnp.einsum('az,xya->xyz', table_z, solved, precision=highest)
    grad_x = 0.5 * (jnp.roll(pressure, -1, 0) - jnp.roll(pressure, 1, 0))
    grad_y = 0.5 * (jnp.roll(pressure, -1, 1) - jnp.roll(pressure, 1, 1))
    grad_z = 0.5 * (depth_next(pressure) - depth_prev(pressure))
    velocity_out = velocity - jnp.stack([grad_x, grad_y, grad_z])
    return (scalars_out, velocity_out)
```

```python
import functools
import math

import jax
import jax.numpy as jnp
import numpy as np
from jax import lax
from jax.experimental import pallas as pl
from jax.experimental.pallas import tpu as pltpu
from jax.sharding import PartitionSpec as P

time_step = 0.25


def with_halo(block, sides, width):
    for axis, dim in sides:
        count = lax.axis_size(axis)
        forward = [(i, i + 1) for i in range(count - 1)]
        forward.append((count - 1, 0))
        backward = [(target, source) for source, target in forward]
        low = lax.ppermute(
            lax.slice_in_dim(block, block.shape[dim] - width, None, axis=dim), axis, forward
        )
        high = lax.ppermute(lax.slice_in_dim(block, 0, width, axis=dim), axis, backward)
        block = jnp.concatenate([low, block, high], axis=dim)
    return block


def hartley_table(length):
    position = jnp.arange(length, dtype=jnp.int32)
    product = position[:, None] * position[None, :] % length
    phase_angle = 2.0 * math.pi / length * product.astype(jnp.float32)
    return (jnp.cos(phase_angle) + jnp.sin(phase_angle)) / math.sqrt(length)


def cosine_table(length):
    position = jnp.arange(length, dtype=jnp.int32)
    product = position[:, None] * (2 * position[None, :] + 1) % (4 * length)
    phase_angle = math.pi / (2 * length) * product.astype(jnp.float32)
    weight = jnp.where(position == 0, math.sqrt(1.0 / length), math.sqrt(2.0 / length)).astype(
        jnp.float32
    )
    return weight[:, None] * jnp.cos(phase_angle)


def depth_next(values):
    return jnp.concatenate([values[..., 1:], values[..., -1:]], -1)


def depth_prev(values):
    return jnp.concatenate([values[..., :1], values[..., :-1]], -1)


def transport_rate(field_pad, flow_pad):
    center = field_pad[:, 1:-1, 1:-1]
    x_next = field_pad[:, 2:, 1:-1]
    x_prev = field_pad[:, :-2, 1:-1]
    y_next = field_pad[:, 1:-1, 2:]
    y_prev = field_pad[:, 1:-1, :-2]
    z_next = depth_next(center)
    z_prev = depth_prev(center)
    coefficient = flow_pad[3, 1:-1, 1:-1]
    advection = (
        flow_pad[0, 1:-1, 1:-1] * (x_next - x_prev) * 0.5
        + flow_pad[1, 1:-1, 1:-1] * (y_next - y_prev) * 0.5
        + flow_pad[2, 1:-1, 1:-1] * (z_next - z_prev) * 0.5
    )
    diffusion = 0.5 * (coefficient + flow_pad[3, 2:, 1:-1]) * (x_next - center) - 0.5 * (
        coefficient + flow_pad[3, :-2, 1:-1]
    ) * (center - x_prev)
    diffusion = (
        diffusion
        + 0.5 * (coefficient + flow_pad[3, 1:-1, 2:]) * (y_next - center)
        - 0.5 * (coefficient + flow_pad[3, 1:-1, :-2]) * (center - y_prev)
    )
    diffusion = (
        diffusion
        + 0.5 * (coefficient + depth_next(coefficient)) * (z_next - center)
        - 0.5 * (coefficient + depth_prev(coefficient)) * (center - z_prev)
    )
    return diffusion - advection


def network(blocks, w_in, w_mid, w_out):
    block_count = blocks.shape[0]
    bundle_size = 8
    padded_count = -(-block_count // bundle_size) * bundle_size

    def evaluate(bundle):
        hidden_one = jnp.einsum("hn,bnz->bhz", w_in, bundle, preferred_element_type=jnp.float32)
        hidden_one = jax.nn.gelu(hidden_one).astype(jnp.bfloat16)
        hidden_two = jnp.einsum(
            "kh,bhz->bkz", w_mid, hidden_one, preferred_element_type=jnp.float32
        )
        hidden_two = jax.nn.gelu(hidden_two).astype(jnp.bfloat16)
        return jnp.einsum("nk,bkz->bnz", w_out, hidden_two, preferred_element_type=jnp.float32)

    reaction = lax.map(
        evaluate, blocks.reshape((padded_count // bundle_size, bundle_size) + blocks.shape[1:])
    )
    return reaction.reshape((padded_count,) + reaction.shape[2:])


def solve_modes(spectrum, start_y, start_z, total_x, total_y, total_z):
    mode_x = jnp.arange(spectrum.shape[0], dtype=jnp.int32)
    mode_y = start_y + jnp.arange(spectrum.shape[1], dtype=jnp.int32)
    mode_z = start_z + jnp.arange(spectrum.shape[2], dtype=jnp.int32)
    eigen_x = 2.0 - 2.0 * jnp.cos(2.0 * math.pi / total_x * mode_x.astype(jnp.float32))
    eigen_y = 2.0 - 2.0 * jnp.cos(2.0 * math.pi / total_y * mode_y.astype(jnp.float32))
    eigen_z = 2.0 - 2.0 * jnp.cos(math.pi / total_z * mode_z.astype(jnp.float32))
    eigen = eigen_x[:, None, None] + eigen_y[None, :, None] + eigen_z[None, None, :]
    anchor = (
        (mode_x[:, None, None] == 0) & (mode_y[None, :, None] == 0) & (mode_z[None, None, :] == 0)
    ).astype(jnp.float32)
    return -spectrum * (1.0 - anchor) / (eigen + anchor)


def shards(scalars, velocity, diffusivity, burn_list, w_in, w_mid, w_out):
    channels = scalars.shape[0]
    joined = jnp.concatenate([scalars, velocity, diffusivity[None]], 0)
    padded = with_halo(joined, (("gx", 1), ("gy", 2)), 1)
    field_pad = padded[:channels]
    inner_flow = padded[channels:]
    section_one = scalars + time_step * transport_rate(field_pad, inner_flow)
    section_pad = with_halo(section_one, (("gx", 1), ("gy", 2)), 1)
    transported = 0.5 * scalars + 0.5 * (
        section_one + time_step * transport_rate(section_pad, inner_flow)
    )
    divergence = 0.5 * (inner_flow[0, 2:, 1:-1] - inner_flow[0, :-2, 1:-1])
    divergence = divergence + 0.5 * (inner_flow[1, 1:-1, 2:] - inner_flow[1, 1:-1, :-2])
    vertical = inner_flow[2, 1:-1, 1:-1]
    divergence = divergence + 0.5 * (depth_next(vertical) - depth_prev(vertical))
    highest = lax.Precision.HIGHEST
    cells_x, cells_y, depth = divergence.shape
    total_x = cells_x * lax.axis_size("gx")
    total_y = cells_y * lax.axis_size("gy")
    table_x = hartley_table(total_x)
    table_y = hartley_table(total_y)
    table_z = cosine_table(depth)
    spectrum = jnp.einsum("az,xyz->xya", table_z, divergence, precision=highest)
    along_y = lax.all_to_all(spectrum, "gy", split_axis=2, concat_axis=1, tiled=True)
    along_y = jnp.einsum("by,xyz->xbz", table_y, along_y, precision=highest)
    along_x = lax.all_to_all(
        along_y.astype(jnp.bfloat16), "gx", split_axis=1, concat_axis=0, tiled=True
    ).astype(along_y.dtype)
    along_x = jnp.einsum("cx,xyz->cyz", table_x, along_x, precision=highest)
    solved = solve_modes(
        along_x,
        lax.axis_index("gx") * along_x.shape[1],
        lax.axis_index("gy") * along_x.shape[2],
        total_x,
        total_y,
        depth,
    )
    solved = jnp.einsum("cx,xyz->cyz", table_x, solved, precision=highest)
    solved = lax.all_to_all(solved, "gx", split_axis=0, concat_axis=1, tiled=True)
    solved = jnp.einsum("by,xyz->xbz", table_y, solved, precision=highest)
    solved = lax.all_to_all(solved, "gy", split_axis=1, concat_axis=2, tiled=True)
    pressure = jnp.einsum("az,xya->xyz", table_z, solved, precision=highest)
    pressure_pad = with_halo(pressure, (("gx", 0), ("gy", 1)), 1)
    grad_x = 0.5 * (pressure_pad[2:, 1:-1] - pressure_pad[:-2, 1:-1])
    grad_y = 0.5 * (pressure_pad[1:-1, 2:] - pressure_pad[1:-1, :-2])
    grad_z = 0.5 * (depth_next(pressure) - depth_prev(pressure))
    velocity_out = velocity - jnp.stack([grad_x, grad_y, grad_z])
    block_total = cells_x * cells_y
    flat_blocks = transported.reshape(channels, block_total, depth)
    listed = burn_list.reshape(-1)
    picked = jnp.take(flat_blocks, jnp.minimum(listed, block_total - 1), axis=1)
    chosen = jnp.transpose(picked, (1, 0, 2)).astype(jnp.bfloat16)
    own_rates = network(chosen, w_in, w_mid, w_out)
    updated = flat_blocks.at[:, listed].add(jnp.transpose(own_rates, (1, 0, 2)), mode="drop")
    scalars_out = updated.reshape(transported.shape)
    return (scalars_out, velocity_out)


MESH = pl.DeviceIdType.MESH
BUNDLE = 8


def hartley_np(length):
    product = np.outer(np.arange(length), np.arange(length)) % length
    angle = 2.0 * np.pi / length * product
    return (np.cos(angle) + np.sin(angle)) / np.sqrt(length)


def cosine_np(length):
    k = np.arange(length)
    angle = np.pi / (2 * length) * (np.outer(k, 2 * k + 1) % (4 * length))
    weight = np.where(k == 0, np.sqrt(1.0 / length), np.sqrt(2.0 / length))
    return weight[:, None] * np.cos(angle)


def split_np(table):
    high = table.astype(jnp.bfloat16)
    low = (table - high.astype(np.float64)).astype(jnp.bfloat16)
    return high, low


def split(value):
    high = value.astype(jnp.bfloat16)
    return high, (value - high.astype(jnp.float32)).astype(jnp.bfloat16)


def dot3(a, b, dims=((1,), (0,))):
    run = lambda p, q: lax.dot_general(p, q, (dims, ((), ())), preferred_element_type=jnp.float32)
    return run(a[0], b[0]) + (run(a[1], b[0]) + run(a[0], b[1]))


def z_neighbours(f):
    axis = f.ndim - 1
    depth = f.shape[axis]
    z = lax.broadcasted_iota(jnp.int32, f.shape, axis)
    after = jnp.where(z == depth - 1, f, pltpu.roll(f, depth - 1, axis))
    before = jnp.where(z == 0, f, pltpu.roll(f, 1, axis))
    return after, before


def y_neighbours(f, low, high):
    count = f.shape[1]
    y = lax.broadcasted_iota(jnp.int32, f.shape, 1)
    after = jnp.where(y == count - 1, high[:, None, :], pltpu.roll(f, count - 1, 1))
    before = jnp.where(y == 0, low[:, None, :], pltpu.roll(f, 1, 1))
    return after, before


def x_neighbours(f, low, high):
    after = jnp.concatenate([f[1:], high[None]], 0)
    before = jnp.concatenate([low[None], f[:-1]], 0)
    return after, before


def step_kernel(
    ngx, ngy,
    scal, vel, dif, minv, cz_h, cz_l, ty_h, ty_l, tx_h, tx_l,
    out, vout,
    xsend, ysend, xrecv, yrecv,
    x2send, y2send, x2recv, y2recv,
    psx, psy, prx, pry,
    coef, section, asend, arecv, bsend, brecv, plane, modes,
    h_sem, h2_sem, p_sem, a_ssem, a_rsem, b_ssem, b_rsem,
):
    channels, cx, cy, nz = scal.shape
    n = ngx * ngy
    kc = nz // n
    i = lax.axis_index("gx")
    j = lax.axis_index("gy")
    me = i * ngy + j
    up_x = (lax.rem(i + 1, ngx), j)
    down_x = (lax.rem(i + ngx - 1, ngx), j)
    up_y = (i, lax.rem(j + 1, ngy))
    down_y = (i, lax.rem(j + ngy - 1, ngy))

    barrier = pltpu.get_barrier_semaphore()

    def greet(off, carry):
        d = lax.rem(me + off, n)
        pl.semaphore_signal(barrier, inc=1, device_id=(d // ngy, lax.rem(d, ngy)), device_id_type=MESH)
        return carry

    lax.fori_loop(1, n, greet, 0)

    xsend[0, :channels] = scal[:, cx - 1]
    xsend[1, :channels] = scal[:, 0]
    ysend[0, :channels] = scal[:, :, cy - 1, :]
    ysend[1, :channels] = scal[:, :, 0, :]
    xsend[0, channels:channels + 3] = vel[:, cx - 1]
    xsend[1, channels:channels + 3] = vel[:, 0]
    ysend[0, channels:channels + 3] = vel[:, :, cy - 1, :]
    ysend[1, channels:channels + 3] = vel[:, :, 0, :]
    xsend[0, channels + 3] = dif[cx - 1]
    xsend[1, channels + 3] = dif[0]
    ysend[0, channels + 3] = dif[:, cy - 1, :]
    ysend[1, channels + 3] = dif[:, 0, :]
    pl.semaphore_wait(barrier, n - 1)

    def halo(xs, ys, xr, yr, sems):
        copies = []
        plan = ((xs, xr, 0, up_x), (xs, xr, 1, down_x), (ys, yr, 0, up_y), (ys, yr, 1, down_y))
        for at, (s, r, side, target) in enumerate(plan):
            copy = pltpu.make_async_remote_copy(
                src_ref=s.at[side], dst_ref=r.at[side], send_sem=sems.at[0, at],
                recv_sem=sems.at[1, at], device_id=target, device_id_type=MESH,
            )
            copy.start()
            copies.append(copy)
        return copies

    def everyone(send, recv, ssem, rsem):
        def go(off, carry):
            d = lax.rem(me + off, n)
            pltpu.make_async_remote_copy(
                src_ref=send.at[d], dst_ref=recv.at[me], send_sem=ssem.at[d], recv_sem=rsem.at[me],
                device_id=(d // ngy, lax.rem(d, ngy)), device_id_type=MESH,
            ).start()
            return carry

        lax.fori_loop(1, n, go, 0)
        recv[me] = send[me]

    def everyone_wait(send, recv, ssem, rsem):
        def go(off, carry):
            d = lax.rem(me + off, n)
            copy = pltpu.make_async_remote_copy(
                src_ref=send.at[d], dst_ref=recv.at[d], send_sem=ssem.at[d], recv_sem=rsem.at[d],
                device_id=(d // ngy, lax.rem(d, ngy)), device_id_type=MESH,
            )
            copy.wait_send()
            copy.wait_recv()
            return carry

        lax.fori_loop(1, n, go, 0)

    for copy in halo(xsend, ysend, xrecv, yrecv, h_sem):
        copy.wait()

    u, v, w = vel[0], vel[1], vel[2]
    un, up = x_neighbours(u, xrecv[0, channels], xrecv[1, channels])
    vn, vp = y_neighbours(v, yrecv[0, channels + 1], yrecv[1, channels + 1])
    wn, wp = z_neighbours(w)
    div = 0.5 * (un - up) + 0.5 * (vn - vp) + 0.5 * (wn - wp)
    div = div.reshape(cx * cy, nz)
    spec = dot3((cz_h[...], cz_l[...]), split(div), ((1,), (1,)))
    for d in range(n):
        asend[d] = spec[d * kc:(d + 1) * kc]
    everyone(asend, arecv, a_ssem, a_rsem)

    k = dif[...]
    kxn, kxp = x_neighbours(k, xrecv[0, channels + 3], xrecv[1, channels + 3])
    kyn, kyp = y_neighbours(k, yrecv[0, channels + 3], yrecv[1, channels + 3])
    kzn, kzp = z_neighbours(k)
    half = 0.5 * time_step
    total = None
    for at, (nb, flow) in enumerate(((kxn, -u), (kxp, u), (kyn, -v), (kyp, v), (kzn, -w), (kzp, w))):
        face = k + nb
        coef[at] = half * (face + flow)
        total = face if total is None else total + face
    coef[6] = half * total

    def advance(f, xl, xh, yl, yh):
        xn, xp = x_neighbours(f, xl, xh)
        rate = coef[0] * xn + coef[1] * xp - coef[6] * f
        yn, yp = y_neighbours(f, yl, yh)
        rate = rate + (coef[2] * yn + coef[3] * yp)
        zn, zp = z_neighbours(f)
        return f + (rate + (coef[4] * zn + coef[5] * zp))

    def first(c, carry):
        s = advance(scal[c], xrecv[0, c], xrecv[1, c], yrecv[0, c], yrecv[1, c])
        section[c] = s
        x2send[0, c] = s[cx - 1]
        x2send[1, c] = s[0]
        y2send[0, c] = s[:, cy - 1, :]
        y2send[1, c] = s[:, 0, :]
        return carry

    lax.fori_loop(0, channels, first, 0)
    second_halo = halo(x2send, y2send, x2recv, y2recv, h2_sem)

    everyone_wait(asend, arecv, a_ssem, a_rsem)
    for d in range(n):
        a, b = divmod(d, ngy)
        plane[a * kc:(a + 1) * kc, b * cx * cy:(b + 1) * cx * cy] = arecv[d]
    ny = cy * ngy
    rows = ngx * kc
    table_y = (ty_h[...], ty_l[...])
    table_x = (tx_h[...], tx_l[...])
    along = dot3(split(plane[...]), table_y)
    along = jnp.concatenate([along[:, a * ny:(a + 1) * ny] for a in range(cx)], 0)
    along = dot3(table_x, split(along)) * minv[...]
    along = dot3(table_x, split(along))
    along = jnp.concatenate([along[a * rows:(a + 1) * rows] for a in range(cx)], 1)
    along = dot3(split(along), table_y, ((1,), (1,)))
    for d in range(n):
        a, b = divmod(d, ngy)
        bsend[d] = along[a * kc:(a + 1) * kc, b * cx * cy:(b + 1) * cx * cy]
    everyone(bsend, brecv, b_ssem, b_rsem)

    for copy in second_halo:
        copy.wait()

    def second(c, carry):
        s = advance(section[c], x2recv[0, c], x2recv[1, c], y2recv[0, c], y2recv[1, c])
        out[c] = 0.5 * scal[c] + 0.5 * s
        return carry

    lax.fori_loop(0, channels, second, 0)

    everyone_wait(bsend, brecv, b_ssem, b_rsem)
    for d in range(n):
        modes[d * kc:(d + 1) * kc] = brecv[d]
    pressure = dot3(split(modes[...].T), (cz_h[...], cz_l[...])).reshape(cx, cy, nz)
    psx[0] = pressure[cx - 1]
    psx[1] = pressure[0]
    psy[0] = pressure[:, cy - 1, :]
    psy[1] = pressure[:, 0, :]
    last = halo(psx, psy, prx, pry, p_sem)
    zn, zp = z_neighbours(pressure)
    vout[2] = vel[2] - 0.5 * (zn - zp)
    for copy in last:
        copy.wait()
    xn, xp = x_neighbours(pressure, prx[0], prx[1])
    vout[0] = vel[0] - 0.5 * (xn - xp)
    yn, yp = y_neighbours(pressure, pry[0], pry[1])
    vout[1] = vel[1] - 0.5 * (yn - yp)


def step_call(ngx, ngy, scalars, velocity, diffusivity):
    channels, cx, cy, nz = scalars.shape
    n = ngx * ngy
    kc = nz // n
    nx, ny = cx * ngx, cy * ngy
    hx, hy = hartley_np(nx), hartley_np(ny)
    ty = np.einsum("ab,cjy->jaybc", np.eye(cx), hy.reshape(ny, ngy, cy)).reshape(ngy * cx * cy, cx * ny)
    order = (np.arange(ngx)[None, :] * cx + np.arange(cx)[:, None]).reshape(-1)
    tx = np.kron(hx[np.ix_(order, order)], np.eye(kc))
    ex = np.repeat(2.0 - 2.0 * np.cos(2.0 * np.pi / nx * order), kc)
    ey = 2.0 - 2.0 * np.cos(2.0 * np.pi / ny * np.arange(ny))
    exy = (ex[:, None] + ey[None, :]).astype(np.float32)
    ez = 2.0 - 2.0 * np.cos(np.pi / nz * np.arange(nz))
    ez = np.tile(ez.reshape(n, 1, kc), (1, nx, 1)).reshape(n, nx * kc).astype(np.float32)
    me = lax.axis_index("gx") * ngy + lax.axis_index("gy")
    eigen = jnp.asarray(exy) + lax.dynamic_slice_in_dim(jnp.asarray(ez), me, 1, 0)[0][:, None]
    minv = jnp.where(eigen == 0.0, 0.0, -1.0 / jnp.where(eigen == 0.0, 1.0, eigen))
    tables = [jnp.asarray(t) for pair in (split_np(cosine_np(nz)), split_np(ty), split_np(tx)) for t in pair]
    f32 = jnp.float32
    vm = pl.BlockSpec(memory_space=pltpu.VMEM)
    halo_scratch = lambda c: [pltpu.VMEM((2, c, cy, nz), f32), pltpu.VMEM((2, c, cx, nz), f32)]
    face_scratch = [pltpu.VMEM((2, cy, nz), f32), pltpu.VMEM((2, cx, nz), f32)]
    chunk = pltpu.VMEM((n, kc, cx * cy), f32)
    dma = pltpu.SemaphoreType.DMA
    return pl.pallas_call(
        functools.partial(step_kernel, ngx, ngy),
        out_shape=(jax.ShapeDtypeStruct(scalars.shape, f32), jax.ShapeDtypeStruct(velocity.shape, f32)),
        in_specs=[vm] * 10,
        out_specs=(vm, vm),
        scratch_shapes=halo_scratch(channels + 4) * 2 + halo_scratch(channels) * 2 + face_scratch * 2 + [
            pltpu.VMEM((7, cx, cy, nz), f32), pltpu.VMEM(scalars.shape, f32),
            chunk, chunk, chunk, chunk,
            pltpu.VMEM((ngx * kc, ngy * cx * cy), f32), pltpu.VMEM((nz, cx * cy), f32),
            dma((2, 4)), dma((2, 4)), dma((2, 4)), dma((n,)), dma((n,)), dma((n,)), dma((n,)),
        ],
        compiler_params=pltpu.CompilerParams(
            collective_id=0, has_side_effects=True, vmem_limit_bytes=40 * 1024 * 1024
        ),
    )(scalars, velocity, diffusivity, minv, *tables)


def gelu(x):
    c = math.sqrt(2.0 / math.pi)
    inner = x * (c + (c * 0.044715) * (x * x))
    h = 0.5 * x
    return h + h * jnp.tanh(inner)


def chemistry_kernel(channels, listed, fields, w_in, w_mid, w_out, out):
    total = fields.shape[0] // channels
    out[...] = fields[...]
    count = listed.shape[0]
    width = fields.shape[1]
    f32 = jnp.float32

    def go(g, carry):
        columns = [listed[g * BUNDLE + s] for s in range(BUNDLE)]

        @pl.when(columns[0] < total)
        def _():
            parts = [
                fields[pl.ds(jnp.minimum(c, total - 1), channels, stride=total), :] for c in columns
            ]
            feed = jnp.concatenate(parts, 1).astype(jnp.bfloat16)
            one = gelu(jnp.dot(w_in[...], feed, preferred_element_type=f32)).astype(jnp.bfloat16)
            two = gelu(jnp.dot(w_mid[...], one, preferred_element_type=f32)).astype(jnp.bfloat16)
            rate = jnp.dot(w_out[...], two, preferred_element_type=f32)
            for s, c in enumerate(columns):
                @pl.when(c < total)
                def _():
                    out[pl.ds(c, channels, stride=total), :] = (
                        parts[s] + rate[:, s * width:(s + 1) * width]
                    )

        return carry

    lax.fori_loop(0, count // BUNDLE, go, 0)


def chemistry(transported, burn_list, w_in, w_mid, w_out):
    channels, cx, cy, nz = transported.shape
    fields = transported.reshape(channels * cx * cy, nz)
    vm = pl.BlockSpec(memory_space=pltpu.VMEM)
    result = pl.pallas_call(
        functools.partial(chemistry_kernel, channels),
        out_shape=jax.ShapeDtypeStruct(fields.shape, jnp.float32),
        in_specs=[pl.BlockSpec(memory_space=pltpu.SMEM)] + [vm] * 4,
        out_specs=vm,
        compiler_params=pltpu.CompilerParams(vmem_limit_bytes=40 * 1024 * 1024),
    )(burn_list.reshape(-1), fields, w_in, w_mid, w_out)
    return result.reshape(transported.shape)


def fast_shards(scalars, velocity, diffusivity, burn_list, w_in, w_mid, w_out):
    ngx, ngy = lax.axis_size("gx"), lax.axis_size("gy")
    transported, velocity_out = step_call(ngx, ngy, scalars, velocity, diffusivity)
    return chemistry(transported, burn_list, w_in, w_mid, w_out), velocity_out


def local_shards(scalars, velocity, diffusivity, *rest):
    depth = scalars.shape[-1]
    devices = lax.axis_size("gx") * lax.axis_size("gy")
    plan = fast_shards if depth % devices == 0 else shards
    return plan(scalars, velocity, diffusivity, *rest)


def solution(mesh):
    in_specs = (
        P(None, "gx", "gy", None),
        P(None, "gx", "gy", None),
        P("gx", "gy", None),
        P("gx", "gy", None),
        P(),
        P(),
        P(),
    )
    out_specs = (P(None, "gx", "gy", None), P(None, "gx", "gy", None))
    return jax.shard_map(local_shards, mesh=mesh, in_specs=in_specs, out_specs=out_specs, check_vma=False)
```

```python
import functools
import math

import jax
import jax.numpy as jnp
import numpy as np
from jax import lax
from jax.experimental import pallas as pl
from jax.experimental.pallas import tpu as pltpu
from jax.sharding import PartitionSpec as P

time_step = 0.25


def with_halo(block, sides, width):
    for axis, dim in sides:
        count = lax.axis_size(axis)
        forward = [(i, i + 1) for i in range(count - 1)]
        forward.append((count - 1, 0))
        backward = [(target, source) for source, target in forward]
        low = lax.ppermute(
            lax.slice_in_dim(block, block.shape[dim] - width, None, axis=dim), axis, forward
        )
        high = lax.ppermute(lax.slice_in_dim(block, 0, width, axis=dim), axis, backward)
        block = jnp.concatenate([low, block, high], axis=dim)
    return block


def hartley_table(length):
    position = jnp.arange(length, dtype=jnp.int32)
    product = position[:, None] * position[None, :] % length
    phase_angle = 2.0 * math.pi / length * product.astype(jnp.float32)
    return (jnp.cos(phase_angle) + jnp.sin(phase_angle)) / math.sqrt(length)


def cosine_table(length):
    position = jnp.arange(length, dtype=jnp.int32)
    product = position[:, None] * (2 * position[None, :] + 1) % (4 * length)
    phase_angle = math.pi / (2 * length) * product.astype(jnp.float32)
    weight = jnp.where(position == 0, math.sqrt(1.0 / length), math.sqrt(2.0 / length)).astype(
        jnp.float32
    )
    return weight[:, None] * jnp.cos(phase_angle)


def depth_next(values):
    return jnp.concatenate([values[..., 1:], values[..., -1:]], -1)


def depth_prev(values):
    return jnp.concatenate([values[..., :1], values[..., :-1]], -1)


def transport_rate(field_pad, flow_pad):
    center = field_pad[:, 1:-1, 1:-1]
    x_next = field_pad[:, 2:, 1:-1]
    x_prev = field_pad[:, :-2, 1:-1]
    y_next = field_pad[:, 1:-1, 2:]
    y_prev = field_pad[:, 1:-1, :-2]
    z_next = depth_next(center)
    z_prev = depth_prev(center)
    coefficient = flow_pad[3, 1:-1, 1:-1]
    advection = (
        flow_pad[0, 1:-1, 1:-1] * (x_next - x_prev) * 0.5
        + flow_pad[1, 1:-1, 1:-1] * (y_next - y_prev) * 0.5
        + flow_pad[2, 1:-1, 1:-1] * (z_next - z_prev) * 0.5
    )
    diffusion = 0.5 * (coefficient + flow_pad[3, 2:, 1:-1]) * (x_next - center) - 0.5 * (
        coefficient + flow_pad[3, :-2, 1:-1]
    ) * (center - x_prev)
    diffusion = (
        diffusion
        + 0.5 * (coefficient + flow_pad[3, 1:-1, 2:]) * (y_next - center)
        - 0.5 * (coefficient + flow_pad[3, 1:-1, :-2]) * (center - y_prev)
    )
    diffusion = (
        diffusion
        + 0.5 * (coefficient + depth_next(coefficient)) * (z_next - center)
        - 0.5 * (coefficient + depth_prev(coefficient)) * (center - z_prev)
    )
    return diffusion - advection


def network(blocks, w_in, w_mid, w_out):
    block_count = blocks.shape[0]
    bundle_size = 8
    padded_count = -(-block_count // bundle_size) * bundle_size

    def evaluate(bundle):
        hidden_one = jnp.einsum("hn,bnz->bhz", w_in, bundle, preferred_element_type=jnp.float32)
        hidden_one = jax.nn.gelu(hidden_one).astype(jnp.bfloat16)
        hidden_two = jnp.einsum(
            "kh,bhz->bkz", w_mid, hidden_one, preferred_element_type=jnp.float32
        )
        hidden_two = jax.nn.gelu(hidden_two).astype(jnp.bfloat16)
        return jnp.einsum("nk,bkz->bnz", w_out, hidden_two, preferred_element_type=jnp.float32)

    reaction = lax.map(
        evaluate, blocks.reshape((padded_count // bundle_size, bundle_size) + blocks.shape[1:])
    )
    return reaction.reshape((padded_count,) + reaction.shape[2:])


def solve_modes(spectrum, start_y, start_z, total_x, total_y, total_z):
    mode_x = jnp.arange(spectrum.shape[0], dtype=jnp.int32)
    mode_y = start_y + jnp.arange(spectrum.shape[1], dtype=jnp.int32)
    mode_z = start_z + jnp.arange(spectrum.shape[2], dtype=jnp.int32)
    eigen_x = 2.0 - 2.0 * jnp.cos(2.0 * math.pi / total_x * mode_x.astype(jnp.float32))
    eigen_y = 2.0 - 2.0 * jnp.cos(2.0 * math.pi / total_y * mode_y.astype(jnp.float32))
    eigen_z = 2.0 - 2.0 * jnp.cos(math.pi / total_z * mode_z.astype(jnp.float32))
    eigen = eigen_x[:, None, None] + eigen_y[None, :, None] + eigen_z[None, None, :]
    anchor = (
        (mode_x[:, None, None] == 0) & (mode_y[None, :, None] == 0) & (mode_z[None, None, :] == 0)
    ).astype(jnp.float32)
    return -spectrum * (1.0 - anchor) / (eigen + anchor)


def shards(scalars, velocity, diffusivity, burn_list, w_in, w_mid, w_out):
    channels = scalars.shape[0]
    joined = jnp.concatenate([scalars, velocity, diffusivity[None]], 0)
    padded = with_halo(joined, (("gx", 1), ("gy", 2)), 1)
    field_pad = padded[:channels]
    inner_flow = padded[channels:]
    section_one = scalars + time_step * transport_rate(field_pad, inner_flow)
    section_pad = with_halo(section_one, (("gx", 1), ("gy", 2)), 1)
    transported = 0.5 * scalars + 0.5 * (
        section_one + time_step * transport_rate(section_pad, inner_flow)
    )
    divergence = 0.5 * (inner_flow[0, 2:, 1:-1] - inner_flow[0, :-2, 1:-1])
    divergence = divergence + 0.5 * (inner_flow[1, 1:-1, 2:] - inner_flow[1, 1:-1, :-2])
    vertical = inner_flow[2, 1:-1, 1:-1]
    divergence = divergence + 0.5 * (depth_next(vertical) - depth_prev(vertical))
    highest = lax.Precision.HIGHEST
    cells_x, cells_y, depth = divergence.shape
    total_x = cells_x * lax.axis_size("gx")
    total_y = cells_y * lax.axis_size("gy")
    table_x = hartley_table(total_x)
    table_y = hartley_table(total_y)
    table_z = cosine_table(depth)
    spectrum = jnp.einsum("az,xyz->xya", table_z, divergence, precision=highest)
    along_y = lax.all_to_all(spectrum, "gy", split_axis=2, concat_axis=1, tiled=True)
    along_y = jnp.einsum("by,xyz->xbz", table_y, along_y, precision=highest)
    along_x = lax.all_to_all(
        along_y.astype(jnp.bfloat16), "gx", split_axis=1, concat_axis=0, tiled=True
    ).astype(along_y.dtype)
    along_x = jnp.einsum("cx,xyz->cyz", table_x, along_x, precision=highest)
    solved = solve_modes(
        along_x,
        lax.axis_index("gx") * along_x.shape[1],
        lax.axis_index("gy") * along_x.shape[2],
        total_x,
        total_y,
        depth,
    )
    solved = jnp.einsum("cx,xyz->cyz", table_x, solved, precision=highest)
    solved = lax.all_to_all(solved, "gx", split_axis=0, concat_axis=1, tiled=True)
    solved = jnp.einsum("by,xyz->xbz", table_y, solved, precision=highest)
    solved = lax.all_to_all(solved, "gy", split_axis=1, concat_axis=2, tiled=True)
    pressure = jnp.einsum("az,xya->xyz", table_z, solved, precision=highest)
    pressure_pad = with_halo(pressure, (("gx", 0), ("gy", 1)), 1)
    grad_x = 0.5 * (pressure_pad[2:, 1:-1] - pressure_pad[:-2, 1:-1])
    grad_y = 0.5 * (pressure_pad[1:-1, 2:] - pressure_pad[1:-1, :-2])
    grad_z = 0.5 * (depth_next(pressure) - depth_prev(pressure))
    velocity_out = velocity - jnp.stack([grad_x, grad_y, grad_z])
    block_total = cells_x * cells_y
    flat_blocks = transported.reshape(channels, block_total, depth)
    listed = burn_list.reshape(-1)
    picked = jnp.take(flat_blocks, jnp.minimum(listed, block_total - 1), axis=1)
    chosen = jnp.transpose(picked, (1, 0, 2)).astype(jnp.bfloat16)
    own_rates = network(chosen, w_in, w_mid, w_out)
    updated = flat_blocks.at[:, listed].add(jnp.transpose(own_rates, (1, 0, 2)), mode="drop")
    scalars_out = updated.reshape(transported.shape)
    return (scalars_out, velocity_out)


MESH = pl.DeviceIdType.MESH
BUNDLE = 8


def hartley_np(length):
    product = np.outer(np.arange(length), np.arange(length)) % length
    angle = 2.0 * np.pi / length * product
    return (np.cos(angle) + np.sin(angle)) / np.sqrt(length)


def cosine_np(length):
    k = np.arange(length)
    angle = np.pi / (2 * length) * (np.outer(k, 2 * k + 1) % (4 * length))
    weight = np.where(k == 0, np.sqrt(1.0 / length), np.sqrt(2.0 / length))
    return weight[:, None] * np.cos(angle)


def split_np(table):
    high = table.astype(jnp.bfloat16)
    low = (table - high.astype(np.float64)).astype(jnp.bfloat16)
    return high, low


def split(value):
    high = value.astype(jnp.bfloat16)
    return high, (value - high.astype(jnp.float32)).astype(jnp.bfloat16)


def dot3(a, b, dims=((1,), (0,))):
    run = lambda p, q: lax.dot_general(p, q, (dims, ((), ())), preferred_element_type=jnp.float32)
    return run(a[0], b[0]) + (run(a[1], b[0]) + run(a[0], b[1]))


def z_neighbours(f):
    axis = f.ndim - 1
    depth = f.shape[axis]
    z = lax.broadcasted_iota(jnp.int32, f.shape, axis)
    after = jnp.where(z == depth - 1, f, pltpu.roll(f, depth - 1, axis))
    before = jnp.where(z == 0, f, pltpu.roll(f, 1, axis))
    return after, before


def y_neighbours(f, low, high):
    count = f.shape[1]
    y = lax.broadcasted_iota(jnp.int32, f.shape, 1)
    after = jnp.where(y == count - 1, high[:, None, :], pltpu.roll(f, count - 1, 1))
    before = jnp.where(y == 0, low[:, None, :], pltpu.roll(f, 1, 1))
    return after, before


def x_neighbours(f, low, high):
    after = jnp.concatenate([f[1:], high[None]], 0)
    before = jnp.concatenate([low[None], f[:-1]], 0)
    return after, before


def gelu(x):
    c = math.sqrt(2.0 / math.pi)
    inner = x * (c + (c * 0.044715) * (x * x))
    h = 0.5 * x
    return h + h * jnp.tanh(inner)


def grouped(count, size, body):
    size = size if count % size == 0 else 1

    def go(g, carry):
        for s in range(size):
            body(g * size + s)
        return carry

    lax.fori_loop(0, count // size, go, 0)


def step_kernel(
    ngx, ngy,
    scal_hbm, vel_hbm, dif_hbm, list_hbm, win_hbm, wmid_hbm, wout_hbm,
    exy_hbm, ez_hbm, czh_hbm, czl_hbm, tyh_hbm, tyl_hbm, txh_hbm, txl_hbm,
    out, vout,
    scal, vel, dif, listed, w_in, w_mid, w_out, exy, ez, cz_h, cz_l, ty_h, ty_l, tx_h, tx_l,
    xsend, ysend, xrecv, yrecv,
    x2send, y2send, x2recv, y2recv,
    psx, psy, prx, pry,
    coef, section, asend, arecv, bsend, brecv, plane, modes, feeds, rates,
    in_sem, h_sem, h2_sem, p_sem, a_sem, b_sem,
):
    channels, cx, cy, nz = scal.shape
    n = ngx * ngy
    kc = nz // n
    cells = cx * cy
    slots = listed.shape[1]
    f32, bf16 = jnp.float32, jnp.bfloat16
    i = lax.axis_index("gx")
    j = lax.axis_index("gy")
    me = i * ngy + j
    up_x = (lax.rem(i + 1, ngx), j)
    down_x = (lax.rem(i + ngx - 1, ngx), j)
    up_y = (i, lax.rem(j + 1, ngy))
    down_y = (i, lax.rem(j + ngy - 1, ngy))

    sources = (vel_hbm, dif_hbm, scal_hbm, list_hbm, czh_hbm, czl_hbm, ez_hbm.at[me], exy_hbm,
               tyh_hbm, tyl_hbm, txh_hbm, txl_hbm, win_hbm, wmid_hbm, wout_hbm)
    targets = (vel, dif, scal, listed, cz_h, cz_l, ez, exy,
               ty_h, ty_l, tx_h, tx_l, w_in, w_mid, w_out)
    fetches = [
        pltpu.make_async_copy(a, b, in_sem.at[at]) for at, (a, b) in enumerate(zip(sources, targets))
    ]
    for fetch in fetches:
        fetch.start()

    columns = [lax.rem(j + dj, ngy) for dj in range(ngy)]

    def others(fn):
        for dj in range(1, ngy):
            fn(i, columns[dj])

        def row(di, carry):
            i2 = lax.rem(i + di, ngx)
            for dj in range(ngy):
                fn(i2, columns[dj])
            return carry

        lax.fori_loop(1, ngx, row, 0)

    barrier = pltpu.get_barrier_semaphore()
    others(lambda i2, j2: pl.semaphore_signal(barrier, inc=1, device_id=(i2, j2), device_id_type=MESH))

    for fetch in fetches[:3]:
        fetch.wait()
    xsend[0, :channels] = scal[:, cx - 1]
    xsend[1, :channels] = scal[:, 0]
    ysend[0, :channels] = scal[:, :, cy - 1, :]
    ysend[1, :channels] = scal[:, :, 0, :]
    xsend[0, channels:channels + 3] = vel[:, cx - 1]
    xsend[1, channels:channels + 3] = vel[:, 0]
    ysend[0, channels:channels + 3] = vel[:, :, cy - 1, :]
    ysend[1, channels:channels + 3] = vel[:, :, 0, :]
    xsend[0, channels + 3] = dif[cx - 1]
    xsend[1, channels + 3] = dif[0]
    ysend[0, channels + 3] = dif[:, cy - 1, :]
    ysend[1, channels + 3] = dif[:, 0, :]
    pl.semaphore_wait(barrier, n - 1)

    def halo(xs, ys, xr, yr, sems):
        copies = []
        plan = ((xs, xr, 0, up_x), (xs, xr, 1, down_x), (ys, yr, 0, up_y), (ys, yr, 1, down_y))
        for at, (s, r, side, target) in enumerate(plan):
            copy = pltpu.make_async_remote_copy(
                src_ref=s.at[side], dst_ref=r.at[side], send_sem=sems.at[0, at],
                recv_sem=sems.at[1, at], device_id=target, device_id_type=MESH,
            )
            copy.start()
            copies.append(copy)
        return copies

    def everyone(send, recv, sems):
        def go(i2, j2):
            pltpu.make_async_remote_copy(
                src_ref=send.at[i2 * ngy + j2], dst_ref=recv.at[me], send_sem=sems.at[0],
                recv_sem=sems.at[1], device_id=(i2, j2), device_id_type=MESH,
            ).start()

        others(go)
        recv[me] = send[me]

    def everyone_wait(recv, sems, side):
        part = recv.at[pl.ds(0, n - 1)]
        pltpu.make_async_copy(part, part, sems.at[side]).wait()

    first_halo = halo(xsend, ysend, xrecv, yrecv, h_sem)
    for fetch in fetches[3:6]:
        fetch.wait()
    cell = lax.broadcasted_iota(jnp.int32, (cells, slots), 0)
    put = (cell == listed[...]).astype(f32)
    take = put.T.astype(bf16)
    put = jnp.concatenate([put, put], 1).astype(bf16)
    for copy in first_halo:
        copy.wait()

    u, v, w = vel[0], vel[1], vel[2]
    un, up = x_neighbours(u, xrecv[0, channels], xrecv[1, channels])
    vn, vp = y_neighbours(v, yrecv[0, channels + 1], yrecv[1, channels + 1])
    wn, wp = z_neighbours(w)
    div = 0.5 * (un - up) + 0.5 * (vn - vp) + 0.5 * (wn - wp)
    div = div.reshape(cells, nz)
    spec = dot3((cz_h[...], cz_l[...]), split(div), ((1,), (1,)))
    for d in range(n):
        asend[d] = spec[d * kc:(d + 1) * kc]
    everyone(asend, arecv, a_sem)

    k = dif[...]
    kxn, kxp = x_neighbours(k, xrecv[0, channels + 3], xrecv[1, channels + 3])
    kyn, kyp = y_neighbours(k, yrecv[0, channels + 3], yrecv[1, channels + 3])
    kzn, kzp = z_neighbours(k)
    half = 0.5 * time_step
    total = None
    for at, (nb, flow) in enumerate(((kxn, -u), (kxp, u), (kyn, -v), (kyp, v), (kzn, -w), (kzp, w))):
        face = k + nb
        coef[at] = half * (face + flow)
        total = face if total is None else total + face
    coef[6] = half * total

    def advance(f, xl, xh, yl, yh):
        xn, xp = x_neighbours(f, xl, xh)
        rate = coef[0] * xn + coef[1] * xp - coef[6] * f
        yn, yp = y_neighbours(f, yl, yh)
        rate = rate + (coef[2] * yn + coef[3] * yp)
        zn, zp = z_neighbours(f)
        return f + (rate + (coef[4] * zn + coef[5] * zp))

    def first(c):
        s = advance(scal[c], xrecv[0, c], xrecv[1, c], yrecv[0, c], yrecv[1, c])
        section[c] = s
        x2send[0, c] = s[cx - 1]
        x2send[1, c] = s[0]
        y2send[0, c] = s[:, cy - 1, :]
        y2send[1, c] = s[:, 0, :]

    grouped(channels, 2, first)
    second_halo = halo(x2send, y2send, x2recv, y2recv, h2_sem)

    for fetch in fetches[6:]:
        fetch.wait()
    rows = ngx * kc
    ny = cy * ngy
    eigen = exy[...] + jnp.concatenate([ez[...]] * (cx * rows // ez.shape[0]), 0)
    minv = jnp.where(eigen == 0.0, 0.0, -1.0 / jnp.where(eigen == 0.0, 1.0, eigen))
    everyone_wait(arecv, a_sem, 1)
    for d in range(n):
        a, b = divmod(d, ngy)
        plane[a * kc:(a + 1) * kc, b * cells:(b + 1) * cells] = arecv[d]
    table_y = (ty_h[...], ty_l[...])
    table_x = (tx_h[...], tx_l[...])
    along = dot3(split(plane[...]), table_y)
    along = jnp.concatenate([along[:, a * ny:(a + 1) * ny] for a in range(cx)], 0)
    along = dot3(table_x, split(along)) * minv
    along = dot3(table_x, split(along))
    along = jnp.concatenate([along[a * rows:(a + 1) * rows] for a in range(cx)], 1)
    along = dot3(split(along), table_y, ((1,), (1,)))
    for d in range(n):
        a, b = divmod(d, ngy)
        bsend[d] = along[a * kc:(a + 1) * kc, b * cells:(b + 1) * cells]
    everyone(bsend, brecv, b_sem)

    for copy in second_halo:
        copy.wait()

    def second(c):
        s = advance(section[c], x2recv[0, c], x2recv[1, c], y2recv[0, c], y2recv[1, c])
        t = 0.5 * scal[c] + 0.5 * s
        out[c] = t
        feeds[pl.ds(c * slots, slots), :] = jnp.dot(
            take, t.reshape(cells, nz).astype(bf16), preferred_element_type=f32
        )

    grouped(channels, 2, second)

    def react(g, carry):
        base = g * BUNDLE
        feed = jnp.concatenate(
            [feeds[pl.ds(base + s, channels, stride=slots), :] for s in range(BUNDLE)], 1
        ).astype(bf16)
        one = lax.dot_general(w_in[...], feed, (((0,), (0,)), ((), ())), preferred_element_type=f32)
        one = gelu(one).astype(bf16)
        two = gelu(jnp.dot(w_mid[...], one, preferred_element_type=f32)).astype(bf16)
        rate = jnp.dot(w_out[...], two, preferred_element_type=f32)
        for s in range(BUNDLE):
            rates[pl.ds(base + s, channels, stride=slots), :] = rate[:, s * nz:(s + 1) * nz]
        return carry

    bundles = slots // BUNDLE
    cut_one, cut_two = bundles * 3 // 8, bundles * 6 // 8
    lax.fori_loop(0, cut_one, react, 0)

    everyone_wait(brecv, b_sem, 1)
    for d in range(n):
        modes[d * kc:(d + 1) * kc] = brecv[d]
    pressure = dot3(split(modes[...].T), (cz_h[...], cz_l[...])).reshape(cx, cy, nz)
    psx[0] = pressure[cx - 1]
    psx[1] = pressure[0]
    psy[0] = pressure[:, cy - 1, :]
    psy[1] = pressure[:, 0, :]
    last = halo(psx, psy, prx, pry, p_sem)
    zn, zp = z_neighbours(pressure)
    vout[2] = vel[2] - 0.5 * (zn - zp)
    section[0] = pressure

    lax.fori_loop(cut_one, cut_two, react, 0)

    for copy in last:
        copy.wait()
    pressure = section[0]
    xn, xp = x_neighbours(pressure, prx[0], prx[1])
    vout[0] = vel[0] - 0.5 * (xn - xp)
    yn, yp = y_neighbours(pressure, pry[0], pry[1])
    vout[1] = vel[1] - 0.5 * (yn - yp)

    lax.fori_loop(cut_two, bundles, react, 0)

    def scatter(c):
        parts = jnp.concatenate(split(rates[pl.ds(c * slots, slots), :]), 0)
        added = jnp.dot(put, parts, preferred_element_type=f32)
        out[c] = out[c] + added.reshape(cx, cy, nz)

    grouped(channels, 4, scatter)
    everyone_wait(arecv, a_sem, 0)
    everyone_wait(brecv, b_sem, 0)


def fast_shards(scalars, velocity, diffusivity, burn_list, w_in, w_mid, w_out):
    ngx, ngy = lax.axis_size("gx"), lax.axis_size("gy")
    channels, cx, cy, nz = scalars.shape
    n = ngx * ngy
    kc = nz // n
    nx, ny = cx * ngx, cy * ngy
    hx, hy = hartley_np(nx), hartley_np(ny)
    ty = np.einsum("ab,cjy->jaybc", np.eye(cx), hy.reshape(ny, ngy, cy)).reshape(ngy * cx * cy, cx * ny)
    order = (np.arange(ngx)[None, :] * cx + np.arange(cx)[:, None]).reshape(-1)
    tx = np.kron(hx[np.ix_(order, order)], np.eye(kc))
    ex = np.repeat(2.0 - 2.0 * np.cos(2.0 * np.pi / nx * order), kc)
    ey = 2.0 - 2.0 * np.cos(2.0 * np.pi / ny * np.arange(ny))
    exy = (ex[:, None] + ey[None, :]).astype(np.float32)
    ez = 2.0 - 2.0 * np.cos(np.pi / nz * np.arange(nz))
    ez = np.tile(ez.reshape(n, kc, 1), (1, max(1, 8 // kc), ny)).astype(np.float32)
    tables = [t for pair in (split_np(cosine_np(nz)), split_np(ty), split_np(tx)) for t in pair]
    operands = [
        scalars, velocity, diffusivity, burn_list.reshape(1, -1), w_in.T, w_mid, w_out,
        *(jnp.asarray(t) for t in (exy, ez, *tables)),
    ]
    f32 = jnp.float32
    slots = operands[3].shape[1]
    vm = pl.BlockSpec(memory_space=pltpu.VMEM)
    copies = [pltpu.VMEM(a.shape, a.dtype) for a in operands]
    copies[8] = pltpu.VMEM(ez.shape[1:], f32)
    halo_scratch = lambda c: [pltpu.VMEM((2, c, cy, nz), f32), pltpu.VMEM((2, c, cx, nz), f32)]
    face_scratch = [pltpu.VMEM((2, cy, nz), f32), pltpu.VMEM((2, cx, nz), f32)]
    chunk = pltpu.VMEM((n, kc, cx * cy), f32)
    dma = pltpu.SemaphoreType.DMA
    return pl.pallas_call(
        functools.partial(step_kernel, ngx, ngy),
        out_shape=(jax.ShapeDtypeStruct(scalars.shape, f32), jax.ShapeDtypeStruct(velocity.shape, f32)),
        in_specs=[pl.BlockSpec(memory_space=pl.ANY)] * len(operands),
        out_specs=(vm, vm),
        scratch_shapes=copies + halo_scratch(channels + 4) * 2 + halo_scratch(channels) * 2 + face_scratch * 2 + [
            pltpu.VMEM((7, cx, cy, nz), f32), pltpu.VMEM(scalars.shape, f32),
            chunk, chunk, chunk, chunk,
            pltpu.VMEM((ngx * kc, ngy * cx * cy), f32), pltpu.VMEM((nz, cx * cy), f32),
            pltpu.VMEM((channels * slots, nz), f32), pltpu.VMEM((channels * slots, nz), f32),
            dma((len(operands),)), dma((2, 4)), dma((2, 4)), dma((2, 4)), dma((2,)), dma((2,)),
        ],
        compiler_params=pltpu.CompilerParams(
            collective_id=0, has_side_effects=True, vmem_limit_bytes=60 * 1024 * 1024
        ),
    )(*operands)


def local_shards(scalars, velocity, diffusivity, *rest):
    depth = scalars.shape[-1]
    devices = lax.axis_size("gx") * lax.axis_size("gy")
    whole_chunks = depth % devices == 0 and 8 % (depth // devices) == 0
    plan = fast_shards if whole_chunks else shards
    return plan(scalars, velocity, diffusivity, *rest)


def solution(mesh):
    in_specs = (
        P(None, "gx", "gy", None),
        P(None, "gx", "gy", None),
        P("gx", "gy", None),
        P("gx", "gy", None),
        P(),
        P(),
        P(),
    )
    out_specs = (P(None, "gx", "gy", None), P(None, "gx", "gy", None))
    return jax.shard_map(local_shards, mesh=mesh, in_specs=in_specs, out_specs=out_specs, check_vma=False)
```

```python
import functools
import math

import jax
import jax.numpy as jnp
import numpy as np
from jax import lax
from jax.experimental import pallas as pl
from jax.experimental.pallas import tpu as pltpu
from jax.sharding import PartitionSpec as P

time_step = 0.25


def with_halo(block, sides, width):
    for axis, dim in sides:
        count = lax.axis_size(axis)
        forward = [(i, i + 1) for i in range(count - 1)]
        forward.append((count - 1, 0))
        backward = [(target, source) for source, target in forward]
        low = lax.ppermute(
            lax.slice_in_dim(block, block.shape[dim] - width, None, axis=dim), axis, forward
        )
        high = lax.ppermute(lax.slice_in_dim(block, 0, width, axis=dim), axis, backward)
        block = jnp.concatenate([low, block, high], axis=dim)
    return block


def hartley_table(length):
    position = jnp.arange(length, dtype=jnp.int32)
    product = position[:, None] * position[None, :] % length
    phase_angle = 2.0 * math.pi / length * product.astype(jnp.float32)
    return (jnp.cos(phase_angle) + jnp.sin(phase_angle)) / math.sqrt(length)


def cosine_table(length):
    position = jnp.arange(length, dtype=jnp.int32)
    product = position[:, None] * (2 * position[None, :] + 1) % (4 * length)
    phase_angle = math.pi / (2 * length) * product.astype(jnp.float32)
    weight = jnp.where(position == 0, math.sqrt(1.0 / length), math.sqrt(2.0 / length)).astype(
        jnp.float32
    )
    return weight[:, None] * jnp.cos(phase_angle)


def depth_next(values):
    return jnp.concatenate([values[..., 1:], values[..., -1:]], -1)


def depth_prev(values):
    return jnp.concatenate([values[..., :1], values[..., :-1]], -1)


def transport_rate(field_pad, flow_pad):
    center = field_pad[:, 1:-1, 1:-1]
    x_next = field_pad[:, 2:, 1:-1]
    x_prev = field_pad[:, :-2, 1:-1]
    y_next = field_pad[:, 1:-1, 2:]
    y_prev = field_pad[:, 1:-1, :-2]
    z_next = depth_next(center)
    z_prev = depth_prev(center)
    coefficient = flow_pad[3, 1:-1, 1:-1]
    advection = (
        flow_pad[0, 1:-1, 1:-1] * (x_next - x_prev) * 0.5
        + flow_pad[1, 1:-1, 1:-1] * (y_next - y_prev) * 0.5
        + flow_pad[2, 1:-1, 1:-1] * (z_next - z_prev) * 0.5
    )
    diffusion = 0.5 * (coefficient + flow_pad[3, 2:, 1:-1]) * (x_next - center) - 0.5 * (
        coefficient + flow_pad[3, :-2, 1:-1]
    ) * (center - x_prev)
    diffusion = (
        diffusion
        + 0.5 * (coefficient + flow_pad[3, 1:-1, 2:]) * (y_next - center)
        - 0.5 * (coefficient + flow_pad[3, 1:-1, :-2]) * (center - y_prev)
    )
    diffusion = (
        diffusion
        + 0.5 * (coefficient + depth_next(coefficient)) * (z_next - center)
        - 0.5 * (coefficient + depth_prev(coefficient)) * (center - z_prev)
    )
    return diffusion - advection


def network(blocks, w_in, w_mid, w_out):
    block_count = blocks.shape[0]
    bundle_size = 8
    padded_count = -(-block_count // bundle_size) * bundle_size

    def evaluate(bundle):
        hidden_one = jnp.einsum("hn,bnz->bhz", w_in, bundle, preferred_element_type=jnp.float32)
        hidden_one = jax.nn.gelu(hidden_one).astype(jnp.bfloat16)
        hidden_two = jnp.einsum(
            "kh,bhz->bkz", w_mid, hidden_one, preferred_element_type=jnp.float32
        )
        hidden_two = jax.nn.gelu(hidden_two).astype(jnp.bfloat16)
        return jnp.einsum("nk,bkz->bnz", w_out, hidden_two, preferred_element_type=jnp.float32)

    reaction = lax.map(
        evaluate, blocks.reshape((padded_count // bundle_size, bundle_size) + blocks.shape[1:])
    )
    return reaction.reshape((padded_count,) + reaction.shape[2:])


def solve_modes(spectrum, start_y, start_z, total_x, total_y, total_z):
    mode_x = jnp.arange(spectrum.shape[0], dtype=jnp.int32)
    mode_y = start_y + jnp.arange(spectrum.shape[1], dtype=jnp.int32)
    mode_z = start_z + jnp.arange(spectrum.shape[2], dtype=jnp.int32)
    eigen_x = 2.0 - 2.0 * jnp.cos(2.0 * math.pi / total_x * mode_x.astype(jnp.float32))
    eigen_y = 2.0 - 2.0 * jnp.cos(2.0 * math.pi / total_y * mode_y.astype(jnp.float32))
    eigen_z = 2.0 - 2.0 * jnp.cos(math.pi / total_z * mode_z.astype(jnp.float32))
    eigen = eigen_x[:, None, None] + eigen_y[None, :, None] + eigen_z[None, None, :]
    anchor = (
        (mode_x[:, None, None] == 0) & (mode_y[None, :, None] == 0) & (mode_z[None, None, :] == 0)
    ).astype(jnp.float32)
    return -spectrum * (1.0 - anchor) / (eigen + anchor)


def shards(scalars, velocity, diffusivity, burn_list, w_in, w_mid, w_out):
    channels = scalars.shape[0]
    joined = jnp.concatenate([scalars, velocity, diffusivity[None]], 0)
    padded = with_halo(joined, (("gx", 1), ("gy", 2)), 1)
    field_pad = padded[:channels]
    inner_flow = padded[channels:]
    section_one = scalars + time_step * transport_rate(field_pad, inner_flow)
    section_pad = with_halo(section_one, (("gx", 1), ("gy", 2)), 1)
    transported = 0.5 * scalars + 0.5 * (
        section_one + time_step * transport_rate(section_pad, inner_flow)
    )
    divergence = 0.5 * (inner_flow[0, 2:, 1:-1] - inner_flow[0, :-2, 1:-1])
    divergence = divergence + 0.5 * (inner_flow[1, 1:-1, 2:] - inner_flow[1, 1:-1, :-2])
    vertical = inner_flow[2, 1:-1, 1:-1]
    divergence = divergence + 0.5 * (depth_next(vertical) - depth_prev(vertical))
    highest = lax.Precision.HIGHEST
    cells_x, cells_y, depth = divergence.shape
    total_x = cells_x * lax.axis_size("gx")
    total_y = cells_y * lax.axis_size("gy")
    table_x = hartley_table(total_x)
    table_y = hartley_table(total_y)
    table_z = cosine_table(depth)
    spectrum = jnp.einsum("az,xyz->xya", table_z, divergence, precision=highest)
    along_y = lax.all_to_all(spectrum, "gy", split_axis=2, concat_axis=1, tiled=True)
    along_y = jnp.einsum("by,xyz->xbz", table_y, along_y, precision=highest)
    along_x = lax.all_to_all(
        along_y.astype(jnp.bfloat16), "gx", split_axis=1, concat_axis=0, tiled=True
    ).astype(along_y.dtype)
    along_x = jnp.einsum("cx,xyz->cyz", table_x, along_x, precision=highest)
    solved = solve_modes(
        along_x,
        lax.axis_index("gx") * along_x.shape[1],
        lax.axis_index("gy") * along_x.shape[2],
        total_x,
        total_y,
        depth,
    )
    solved = jnp.einsum("cx,xyz->cyz", table_x, solved, precision=highest)
    solved = lax.all_to_all(solved, "gx", split_axis=0, concat_axis=1, tiled=True)
    solved = jnp.einsum("by,xyz->xbz", table_y, solved, precision=highest)
    solved = lax.all_to_all(solved, "gy", split_axis=1, concat_axis=2, tiled=True)
    pressure = jnp.einsum("az,xya->xyz", table_z, solved, precision=highest)
    pressure_pad = with_halo(pressure, (("gx", 0), ("gy", 1)), 1)
    grad_x = 0.5 * (pressure_pad[2:, 1:-1] - pressure_pad[:-2, 1:-1])
    grad_y = 0.5 * (pressure_pad[1:-1, 2:] - pressure_pad[1:-1, :-2])
    grad_z = 0.5 * (depth_next(pressure) - depth_prev(pressure))
    velocity_out = velocity - jnp.stack([grad_x, grad_y, grad_z])
    block_total = cells_x * cells_y
    flat_blocks = transported.reshape(channels, block_total, depth)
    listed = burn_list.reshape(-1)
    picked = jnp.take(flat_blocks, jnp.minimum(listed, block_total - 1), axis=1)
    chosen = jnp.transpose(picked, (1, 0, 2)).astype(jnp.bfloat16)
    own_rates = network(chosen, w_in, w_mid, w_out)
    updated = flat_blocks.at[:, listed].add(jnp.transpose(own_rates, (1, 0, 2)), mode="drop")
    scalars_out = updated.reshape(transported.shape)
    return (scalars_out, velocity_out)


MESH = pl.DeviceIdType.MESH
BUNDLE = 8


def hartley_np(length):
    product = np.outer(np.arange(length), np.arange(length)) % length
    angle = 2.0 * np.pi / length * product
    return (np.cos(angle) + np.sin(angle)) / np.sqrt(length)


def cosine_np(length):
    k = np.arange(length)
    angle = np.pi / (2 * length) * (np.outer(k, 2 * k + 1) % (4 * length))
    weight = np.where(k == 0, np.sqrt(1.0 / length), np.sqrt(2.0 / length))
    return weight[:, None] * np.cos(angle)


def split_np(table):
    high = table.astype(jnp.bfloat16)
    low = (table - high.astype(np.float64)).astype(jnp.bfloat16)
    return high, low


def split(value):
    high = value.astype(jnp.bfloat16)
    return high, (value - high.astype(jnp.float32)).astype(jnp.bfloat16)


def dot3(a, b, dims=((1,), (0,))):
    run = lambda p, q: lax.dot_general(p, q, (dims, ((), ())), preferred_element_type=jnp.float32)
    return run(a[0], b[0]) + (run(a[1], b[0]) + run(a[0], b[1]))


def z_neighbours(f):
    axis = f.ndim - 1
    depth = f.shape[axis]
    z = lax.broadcasted_iota(jnp.int32, f.shape, axis)
    after = jnp.where(z == depth - 1, f, pltpu.roll(f, depth - 1, axis))
    before = jnp.where(z == 0, f, pltpu.roll(f, 1, axis))
    return after, before


def y_neighbours(f, low, high):
    count = f.shape[1]
    y = lax.broadcasted_iota(jnp.int32, f.shape, 1)
    after = jnp.where(y == count - 1, high[:, None, :], pltpu.roll(f, count - 1, 1))
    before = jnp.where(y == 0, low[:, None, :], pltpu.roll(f, 1, 1))
    return after, before


def x_neighbours(f, low, high):
    after = jnp.concatenate([f[1:], high[None]], 0)
    before = jnp.concatenate([low[None], f[:-1]], 0)
    return after, before


def gelu(x):
    c = math.sqrt(2.0 / math.pi)
    inner = x * (c + (c * 0.044715) * (x * x))
    h = 0.5 * x
    return h + h * jnp.tanh(inner)


def grouped(count, size, body):
    size = size if count % size == 0 else 1

    def go(g, carry):
        for s in range(size):
            body(g * size + s)
        return carry

    lax.fori_loop(0, count // size, go, 0)


def step_kernel(
    ngx, ngy,
    scal_hbm, vel_hbm, dif_hbm, list_hbm, win_hbm, wmid_hbm, wout_hbm,
    exy_hbm, ez_hbm, czh_hbm, czl_hbm, tyh_hbm, tyl_hbm, txh_hbm, txl_hbm,
    out, vout,
    scal, vel, dif, listed, w_in, w_mid, w_out, exy, ez, cz_h, cz_l, ty_h, ty_l, tx_h, tx_l,
    xsend, ysend, xrecv, yrecv,
    x2send, y2send, x2recv, y2recv,
    psx, psy, prx, pry, gsx, gsy, grx, gry,
    coef, section, asend, arecv, bsend, brecv, plane, modes, feeds, rates,
    in_sem, g_sem, h_sem, h2_sem, p_sem, a_sem, b_sem,
):
    channels, cx, cy, nz = scal.shape
    n = ngx * ngy
    kc = nz // n
    cells = cx * cy
    slots = listed.shape[1]
    f32, bf16 = jnp.float32, jnp.bfloat16
    i = lax.axis_index("gx")
    j = lax.axis_index("gy")
    me = i * ngy + j
    up_x = (lax.rem(i + 1, ngx), j)
    down_x = (lax.rem(i + ngx - 1, ngx), j)
    up_y = (i, lax.rem(j + 1, ngy))
    down_y = (i, lax.rem(j + ngy - 1, ngy))

    sources = (vel_hbm, dif_hbm, scal_hbm, list_hbm, czh_hbm, czl_hbm, ez_hbm.at[me], exy_hbm,
               tyh_hbm, tyl_hbm, txh_hbm, txl_hbm, win_hbm, wmid_hbm, wout_hbm)
    targets = (vel, dif, scal, listed, cz_h, cz_l, ez, exy,
               ty_h, ty_l, tx_h, tx_l, w_in, w_mid, w_out)
    fetches = [
        pltpu.make_async_copy(a, b, in_sem.at[at]) for at, (a, b) in enumerate(zip(sources, targets))
    ]
    for fetch in fetches[:3]:
        fetch.start()

    columns = [lax.rem(j + dj, ngy) for dj in range(ngy)]

    def others(fn):
        for dj in range(1, ngy):
            fn(i, columns[dj])

        def row(di, carry):
            i2 = lax.rem(i + di, ngx)
            for dj in range(ngy):
                fn(i2, columns[dj])
            return carry

        lax.fori_loop(1, ngx, row, 0)

    barrier = pltpu.get_barrier_semaphore()
    others(lambda i2, j2: pl.semaphore_signal(barrier, inc=1, device_id=(i2, j2), device_id_type=MESH))

    for fetch in fetches[:2]:
        fetch.wait()
    for side, at in ((0, cx - 1), (1, 0)):
        gsx[side, 0] = vel[0, at]
        gsx[side, 1] = dif[at]
    for side, at in ((0, cy - 1), (1, 0)):
        gsy[side, 0] = vel[1, :, at, :]
        gsy[side, 1] = dif[:, at, :]
    fetches[2].wait()

    def pack(c, f, xs, ys):
        xs[0, c] = f[cx - 1].astype(bf16)
        xs[1, c] = f[0].astype(bf16)
        ys[0, c] = f[:, cy - 1, :].astype(bf16)
        ys[1, c] = f[:, 0, :].astype(bf16)

    grouped(channels, 4, lambda c: pack(c, scal[c], xsend, ysend))
    pl.semaphore_wait(barrier, n - 1)

    def halo(xs, ys, xr, yr, sems):
        copies = []
        plan = ((xs, xr, 0, up_x), (xs, xr, 1, down_x), (ys, yr, 0, up_y), (ys, yr, 1, down_y))
        for at, (s, r, side, target) in enumerate(plan):
            copy = pltpu.make_async_remote_copy(
                src_ref=s.at[side], dst_ref=r.at[side], send_sem=sems.at[0, at],
                recv_sem=sems.at[1, at], device_id=target, device_id_type=MESH,
            )
            copy.start()
            copies.append(copy)
        return copies

    def everyone(send, recv, sems):
        def go(i2, j2):
            pltpu.make_async_remote_copy(
                src_ref=send.at[i2 * ngy + j2], dst_ref=recv.at[me], send_sem=sems.at[0],
                recv_sem=sems.at[1], device_id=(i2, j2), device_id_type=MESH,
            ).start()

        others(go)
        recv[me] = send[me]

    def everyone_wait(recv, sems, side):
        part = recv.at[pl.ds(0, n - 1)]
        pltpu.make_async_copy(part, part, sems.at[side]).wait()

    flow_halo = halo(gsx, gsy, grx, gry, g_sem)
    first_halo = halo(xsend, ysend, xrecv, yrecv, h_sem)
    for fetch in fetches[3:]:
        fetch.start()
    for fetch in fetches[3:6]:
        fetch.wait()
    cell = lax.broadcasted_iota(jnp.int32, (cells, slots), 0)
    put = (cell == listed[...]).astype(f32)
    take = put.T.astype(bf16)
    put = jnp.concatenate([put, put], 1).astype(bf16)
    for copy in flow_halo:
        copy.wait()

    u, v, w = vel[0], vel[1], vel[2]
    un, up = x_neighbours(u, grx[0, 0], grx[1, 0])
    vn, vp = y_neighbours(v, gry[0, 0], gry[1, 0])
    wn, wp = z_neighbours(w)
    div = 0.5 * (un - up) + 0.5 * (vn - vp) + 0.5 * (wn - wp)
    div = div.reshape(cells, nz)
    spec = dot3((cz_h[...], cz_l[...]), split(div), ((1,), (1,)))
    for d in range(n):
        asend[d] = spec[d * kc:(d + 1) * kc]
    everyone(asend, arecv, a_sem)

    k = dif[...]
    kxn, kxp = x_neighbours(k, grx[0, 1], grx[1, 1])
    kyn, kyp = y_neighbours(k, gry[0, 1], gry[1, 1])
    kzn, kzp = z_neighbours(k)
    half = 0.5 * time_step
    total = None
    for at, (nb, flow) in enumerate(((kxn, -u), (kxp, u), (kyn, -v), (kyp, v), (kzn, -w), (kzp, w))):
        face = k + nb
        coef[at] = half * (face + flow)
        total = face if total is None else total + face
    coef[6] = half * total

    def advance(f, c, xr, yr):
        xl, xh, yl, yh = (r[side, c].astype(f32) for r in (xr, yr) for side in (0, 1))
        xn, xp = x_neighbours(f, xl, xh)
        rate = coef[0] * xn + coef[1] * xp - coef[6] * f
        yn, yp = y_neighbours(f, yl, yh)
        rate = rate + (coef[2] * yn + coef[3] * yp)
        zn, zp = z_neighbours(f)
        return f + (rate + (coef[4] * zn + coef[5] * zp))

    for copy in first_halo:
        copy.wait()

    def first(c):
        s = advance(scal[c], c, xrecv, yrecv)
        section[c] = s
        pack(c, s, x2send, y2send)

    grouped(channels, 2, first)
    second_halo = halo(x2send, y2send, x2recv, y2recv, h2_sem)

    for fetch in fetches[6:]:
        fetch.wait()
    rows = ngx * kc
    ny = cy * ngy
    eigen = exy[...] + jnp.concatenate([ez[...]] * (cx * rows // ez.shape[0]), 0)
    minv = jnp.where(eigen == 0.0, 0.0, -1.0 / jnp.where(eigen == 0.0, 1.0, eigen))
    everyone_wait(arecv, a_sem, 1)
    for d in range(n):
        a, b = divmod(d, ngy)
        plane[a * kc:(a + 1) * kc, b * cells:(b + 1) * cells] = arecv[d]
    table_y = (ty_h[...], ty_l[...])
    table_x = (tx_h[...], tx_l[...])
    along = dot3(split(plane[...]), table_y)
    along = jnp.concatenate([along[:, a * ny:(a + 1) * ny] for a in range(cx)], 0)
    along = dot3(table_x, split(along)) * minv
    along = dot3(table_x, split(along))
    along = jnp.concatenate([along[a * rows:(a + 1) * rows] for a in range(cx)], 1)
    along = dot3(split(along), table_y, ((1,), (1,)))
    for d in range(n):
        a, b = divmod(d, ngy)
        bsend[d] = along[a * kc:(a + 1) * kc, b * cells:(b + 1) * cells]
    everyone(bsend, brecv, b_sem)

    for copy in second_halo:
        copy.wait()

    def second(c):
        s = advance(section[c], c, x2recv, y2recv)
        t = 0.5 * scal[c] + 0.5 * s
        out[c] = t
        feeds[pl.ds(c * slots, slots), :] = jnp.dot(
            take, t.reshape(cells, nz).astype(bf16), preferred_element_type=f32
        )

    grouped(channels, 2, second)

    def react(g, carry):
        base = g * BUNDLE
        feed = jnp.concatenate(
            [feeds[pl.ds(base + s, channels, stride=slots), :] for s in range(BUNDLE)], 1
        ).astype(bf16)
        one = lax.dot_general(w_in[...], feed, (((0,), (0,)), ((), ())), preferred_element_type=f32)
        one = gelu(one).astype(bf16)
        two = gelu(jnp.dot(w_mid[...], one, preferred_element_type=f32)).astype(bf16)
        rate = jnp.dot(w_out[...], two, preferred_element_type=f32)
        for s in range(BUNDLE):
            rates[pl.ds(base + s, channels, stride=slots), :] = rate[:, s * nz:(s + 1) * nz]
        return carry

    bundles = slots // BUNDLE
    cut_one, cut_two = bundles * 3 // 8, bundles * 6 // 8
    lax.fori_loop(0, cut_one, react, 0)

    everyone_wait(brecv, b_sem, 1)
    for d in range(n):
        modes[d * kc:(d + 1) * kc] = brecv[d]
    pressure = dot3(split(modes[...].T), (cz_h[...], cz_l[...])).reshape(cx, cy, nz)
    psx[0] = pressure[cx - 1]
    psx[1] = pressure[0]
    psy[0] = pressure[:, cy - 1, :]
    psy[1] = pressure[:, 0, :]
    last = halo(psx, psy, prx, pry, p_sem)
    zn, zp = z_neighbours(pressure)
    vout[2] = vel[2] - 0.5 * (zn - zp)
    section[0] = pressure

    lax.fori_loop(cut_one, cut_two, react, 0)

    for copy in last:
        copy.wait()
    pressure = section[0]
    xn, xp = x_neighbours(pressure, prx[0], prx[1])
    vout[0] = vel[0] - 0.5 * (xn - xp)
    yn, yp = y_neighbours(pressure, pry[0], pry[1])
    vout[1] = vel[1] - 0.5 * (yn - yp)

    lax.fori_loop(cut_two, bundles, react, 0)

    def scatter(c):
        parts = jnp.concatenate(split(rates[pl.ds(c * slots, slots), :]), 0)
        added = jnp.dot(put, parts, preferred_element_type=f32)
        out[c] = out[c] + added.reshape(cx, cy, nz)

    grouped(channels, 4, scatter)
    everyone_wait(arecv, a_sem, 0)
    everyone_wait(brecv, b_sem, 0)


def fast_shards(scalars, velocity, diffusivity, burn_list, w_in, w_mid, w_out):
    ngx, ngy = lax.axis_size("gx"), lax.axis_size("gy")
    channels, cx, cy, nz = scalars.shape
    n = ngx * ngy
    kc = nz // n
    nx, ny = cx * ngx, cy * ngy
    hx, hy = hartley_np(nx), hartley_np(ny)
    ty = np.einsum("ab,cjy->jaybc", np.eye(cx), hy.reshape(ny, ngy, cy)).reshape(ngy * cx * cy, cx * ny)
    order = (np.arange(ngx)[None, :] * cx + np.arange(cx)[:, None]).reshape(-1)
    tx = np.kron(hx[np.ix_(order, order)], np.eye(kc))
    ex = np.repeat(2.0 - 2.0 * np.cos(2.0 * np.pi / nx * order), kc)
    ey = 2.0 - 2.0 * np.cos(2.0 * np.pi / ny * np.arange(ny))
    exy = (ex[:, None] + ey[None, :]).astype(np.float32)
    ez = 2.0 - 2.0 * np.cos(np.pi / nz * np.arange(nz))
    ez = np.tile(ez.reshape(n, kc, 1), (1, max(1, 8 // kc), ny)).astype(np.float32)
    tables = [t for pair in (split_np(cosine_np(nz)), split_np(ty), split_np(tx)) for t in pair]
    operands = [
        scalars, velocity, diffusivity, burn_list.reshape(1, -1), w_in.T, w_mid, w_out,
        *(jnp.asarray(t) for t in (exy, ez, *tables)),
    ]
    f32 = jnp.float32
    slots = operands[3].shape[1]
    vm = pl.BlockSpec(memory_space=pltpu.VMEM)
    copies = [pltpu.VMEM(a.shape, a.dtype) for a in operands]
    copies[8] = pltpu.VMEM(ez.shape[1:], f32)
    halo_scratch = lambda c, t: [pltpu.VMEM((2, c, cy, nz), t), pltpu.VMEM((2, c, cx, nz), t)]
    face_scratch = [pltpu.VMEM((2, cy, nz), f32), pltpu.VMEM((2, cx, nz), f32)]
    chunk = pltpu.VMEM((n, kc, cx * cy), f32)
    dma = pltpu.SemaphoreType.DMA
    return pl.pallas_call(
        functools.partial(step_kernel, ngx, ngy),
        out_shape=(jax.ShapeDtypeStruct(scalars.shape, f32), jax.ShapeDtypeStruct(velocity.shape, f32)),
        in_specs=[pl.BlockSpec(memory_space=pl.ANY)] * len(operands),
        out_specs=(vm, vm),
        scratch_shapes=copies + halo_scratch(channels, jnp.bfloat16) * 4 + face_scratch * 2 + halo_scratch(2, f32) * 2 + [
            pltpu.VMEM((7, cx, cy, nz), f32), pltpu.VMEM(scalars.shape, f32),
            chunk, chunk, chunk, chunk,
            pltpu.VMEM((ngx * kc, ngy * cx * cy), f32), pltpu.VMEM((nz, cx * cy), f32),
            pltpu.VMEM((channels * slots, nz), f32), pltpu.VMEM((channels * slots, nz), f32),
            dma((len(operands),)), dma((2, 4)), dma((2, 4)), dma((2, 4)), dma((2, 4)), dma((2,)), dma((2,)),
        ],
        compiler_params=pltpu.CompilerParams(
            collective_id=0, has_side_effects=True, vmem_limit_bytes=60 * 1024 * 1024
        ),
    )(*operands)


def local_shards(scalars, velocity, diffusivity, *rest):
    depth = scalars.shape[-1]
    devices = lax.axis_size("gx") * lax.axis_size("gy")
    whole_chunks = depth % devices == 0 and 8 % (depth // devices) == 0
    plan = fast_shards if whole_chunks else shards
    return plan(scalars, velocity, diffusivity, *rest)


def solution(mesh):
    in_specs = (
        P(None, "gx", "gy", None),
        P(None, "gx", "gy", None),
        P("gx", "gy", None),
        P("gx", "gy", None),
        P(),
        P(),
        P(),
    )
    out_specs = (P(None, "gx", "gy", None), P(None, "gx", "gy", None))
    return jax.shard_map(local_shards, mesh=mesh, in_specs=in_specs, out_specs=out_specs, check_vma=False)
```

```python
import functools
import math

import jax
import jax.numpy as jnp
import numpy as np
from jax import lax
from jax.experimental import pallas as pl
from jax.experimental.pallas import tpu as pltpu
from jax.sharding import PartitionSpec as P

time_step = 0.25


def with_halo(block, sides, width):
    for axis, dim in sides:
        count = lax.axis_size(axis)
        forward = [(i, i + 1) for i in range(count - 1)]
        forward.append((count - 1, 0))
        backward = [(target, source) for source, target in forward]
        low = lax.ppermute(
            lax.slice_in_dim(block, block.shape[dim] - width, None, axis=dim), axis, forward
        )
        high = lax.ppermute(lax.slice_in_dim(block, 0, width, axis=dim), axis, backward)
        block = jnp.concatenate([low, block, high], axis=dim)
    return block


def hartley_table(length):
    position = jnp.arange(length, dtype=jnp.int32)
    product = position[:, None] * position[None, :] % length
    phase_angle = 2.0 * math.pi / length * product.astype(jnp.float32)
    return (jnp.cos(phase_angle) + jnp.sin(phase_angle)) / math.sqrt(length)


def cosine_table(length):
    position = jnp.arange(length, dtype=jnp.int32)
    product = position[:, None] * (2 * position[None, :] + 1) % (4 * length)
    phase_angle = math.pi / (2 * length) * product.astype(jnp.float32)
    weight = jnp.where(position == 0, math.sqrt(1.0 / length), math.sqrt(2.0 / length)).astype(
        jnp.float32
    )
    return weight[:, None] * jnp.cos(phase_angle)


def depth_next(values):
    return jnp.concatenate([values[..., 1:], values[..., -1:]], -1)


def depth_prev(values):
    return jnp.concatenate([values[..., :1], values[..., :-1]], -1)


def transport_rate(field_pad, flow_pad):
    center = field_pad[:, 1:-1, 1:-1]
    x_next = field_pad[:, 2:, 1:-1]
    x_prev = field_pad[:, :-2, 1:-1]
    y_next = field_pad[:, 1:-1, 2:]
    y_prev = field_pad[:, 1:-1, :-2]
    z_next = depth_next(center)
    z_prev = depth_prev(center)
    coefficient = flow_pad[3, 1:-1, 1:-1]
    advection = (
        flow_pad[0, 1:-1, 1:-1] * (x_next - x_prev) * 0.5
        + flow_pad[1, 1:-1, 1:-1] * (y_next - y_prev) * 0.5
        + flow_pad[2, 1:-1, 1:-1] * (z_next - z_prev) * 0.5
    )
    diffusion = 0.5 * (coefficient + flow_pad[3, 2:, 1:-1]) * (x_next - center) - 0.5 * (
        coefficient + flow_pad[3, :-2, 1:-1]
    ) * (center - x_prev)
    diffusion = (
        diffusion
        + 0.5 * (coefficient + flow_pad[3, 1:-1, 2:]) * (y_next - center)
        - 0.5 * (coefficient + flow_pad[3, 1:-1, :-2]) * (center - y_prev)
    )
    diffusion = (
        diffusion
        + 0.5 * (coefficient + depth_next(coefficient)) * (z_next - center)
        - 0.5 * (coefficient + depth_prev(coefficient)) * (center - z_prev)
    )
    return diffusion - advection


def network(blocks, w_in, w_mid, w_out):
    block_count = blocks.shape[0]
    bundle_size = 8
    padded_count = -(-block_count // bundle_size) * bundle_size

    def evaluate(bundle):
        hidden_one = jnp.einsum("hn,bnz->bhz", w_in, bundle, preferred_element_type=jnp.float32)
        hidden_one = jax.nn.gelu(hidden_one).astype(jnp.bfloat16)
        hidden_two = jnp.einsum(
            "kh,bhz->bkz", w_mid, hidden_one, preferred_element_type=jnp.float32
        )
        hidden_two = jax.nn.gelu(hidden_two).astype(jnp.bfloat16)
        return jnp.einsum("nk,bkz->bnz", w_out, hidden_two, preferred_element_type=jnp.float32)

    reaction = lax.map(
        evaluate, blocks.reshape((padded_count // bundle_size, bundle_size) + blocks.shape[1:])
    )
    return reaction.reshape((padded_count,) + reaction.shape[2:])


def solve_modes(spectrum, start_y, start_z, total_x, total_y, total_z):
    mode_x = jnp.arange(spectrum.shape[0], dtype=jnp.int32)
    mode_y = start_y + jnp.arange(spectrum.shape[1], dtype=jnp.int32)
    mode_z = start_z + jnp.arange(spectrum.shape[2], dtype=jnp.int32)
    eigen_x = 2.0 - 2.0 * jnp.cos(2.0 * math.pi / total_x * mode_x.astype(jnp.float32))
    eigen_y = 2.0 - 2.0 * jnp.cos(2.0 * math.pi / total_y * mode_y.astype(jnp.float32))
    eigen_z = 2.0 - 2.0 * jnp.cos(math.pi / total_z * mode_z.astype(jnp.float32))
    eigen = eigen_x[:, None, None] + eigen_y[None, :, None] + eigen_z[None, None, :]
    anchor = (
        (mode_x[:, None, None] == 0) & (mode_y[None, :, None] == 0) & (mode_z[None, None, :] == 0)
    ).astype(jnp.float32)
    return -spectrum * (1.0 - anchor) / (eigen + anchor)


def shards(scalars, velocity, diffusivity, burn_list, w_in, w_mid, w_out):
    channels = scalars.shape[0]
    joined = jnp.concatenate([scalars, velocity, diffusivity[None]], 0)
    padded = with_halo(joined, (("gx", 1), ("gy", 2)), 1)
    field_pad = padded[:channels]
    inner_flow = padded[channels:]
    section_one = scalars + time_step * transport_rate(field_pad, inner_flow)
    section_pad = with_halo(section_one, (("gx", 1), ("gy", 2)), 1)
    transported = 0.5 * scalars + 0.5 * (
        section_one + time_step * transport_rate(section_pad, inner_flow)
    )
    divergence = 0.5 * (inner_flow[0, 2:, 1:-1] - inner_flow[0, :-2, 1:-1])
    divergence = divergence + 0.5 * (inner_flow[1, 1:-1, 2:] - inner_flow[1, 1:-1, :-2])
    vertical = inner_flow[2, 1:-1, 1:-1]
    divergence = divergence + 0.5 * (depth_next(vertical) - depth_prev(vertical))
    highest = lax.Precision.HIGHEST
    cells_x, cells_y, depth = divergence.shape
    total_x = cells_x * lax.axis_size("gx")
    total_y = cells_y * lax.axis_size("gy")
    table_x = hartley_table(total_x)
    table_y = hartley_table(total_y)
    table_z = cosine_table(depth)
    spectrum = jnp.einsum("az,xyz->xya", table_z, divergence, precision=highest)
    along_y = lax.all_to_all(spectrum, "gy", split_axis=2, concat_axis=1, tiled=True)
    along_y = jnp.einsum("by,xyz->xbz", table_y, along_y, precision=highest)
    along_x = lax.all_to_all(
        along_y.astype(jnp.bfloat16), "gx", split_axis=1, concat_axis=0, tiled=True
    ).astype(along_y.dtype)
    along_x = jnp.einsum("cx,xyz->cyz", table_x, along_x, precision=highest)
    solved = solve_modes(
        along_x,
        lax.axis_index("gx") * along_x.shape[1],
        lax.axis_index("gy") * along_x.shape[2],
        total_x,
        total_y,
        depth,
    )
    solved = jnp.einsum("cx,xyz->cyz", table_x, solved, precision=highest)
    solved = lax.all_to_all(solved, "gx", split_axis=0, concat_axis=1, tiled=True)
    solved = jnp.einsum("by,xyz->xbz", table_y, solved, precision=highest)
    solved = lax.all_to_all(solved, "gy", split_axis=1, concat_axis=2, tiled=True)
    pressure = jnp.einsum("az,xya->xyz", table_z, solved, precision=highest)
    pressure_pad = with_halo(pressure, (("gx", 0), ("gy", 1)), 1)
    grad_x = 0.5 * (pressure_pad[2:, 1:-1] - pressure_pad[:-2, 1:-1])
    grad_y = 0.5 * (pressure_pad[1:-1, 2:] - pressure_pad[1:-1, :-2])
    grad_z = 0.5 * (depth_next(pressure) - depth_prev(pressure))
    velocity_out = velocity - jnp.stack([grad_x, grad_y, grad_z])
    block_total = cells_x * cells_y
    flat_blocks = transported.reshape(channels, block_total, depth)
    listed = burn_list.reshape(-1)
    picked = jnp.take(flat_blocks, jnp.minimum(listed, block_total - 1), axis=1)
    chosen = jnp.transpose(picked, (1, 0, 2)).astype(jnp.bfloat16)
    own_rates = network(chosen, w_in, w_mid, w_out)
    updated = flat_blocks.at[:, listed].add(jnp.transpose(own_rates, (1, 0, 2)), mode="drop")
    scalars_out = updated.reshape(transported.shape)
    return (scalars_out, velocity_out)


MESH = pl.DeviceIdType.MESH
BUNDLE = 8


def hartley_np(length):
    product = np.outer(np.arange(length), np.arange(length)) % length
    angle = 2.0 * np.pi / length * product
    return (np.cos(angle) + np.sin(angle)) / np.sqrt(length)


def cosine_np(length):
    k = np.arange(length)
    angle = np.pi / (2 * length) * (np.outer(k, 2 * k + 1) % (4 * length))
    weight = np.where(k == 0, np.sqrt(1.0 / length), np.sqrt(2.0 / length))
    return weight[:, None] * np.cos(angle)


def split_np(table):
    high = table.astype(jnp.bfloat16)
    low = (table - high.astype(np.float64)).astype(jnp.bfloat16)
    return high, low


def split(value):
    high = value.astype(jnp.bfloat16)
    return high, (value - high.astype(jnp.float32)).astype(jnp.bfloat16)


def dot3(a, b, dims=((1,), (0,))):
    run = lambda p, q: lax.dot_general(p, q, (dims, ((), ())), preferred_element_type=jnp.float32)
    return run(a[0], b[0]) + (run(a[1], b[0]) + run(a[0], b[1]))


def z_neighbours(f):
    axis = f.ndim - 1
    depth = f.shape[axis]
    z = lax.broadcasted_iota(jnp.int32, f.shape, axis)
    after = jnp.where(z == depth - 1, f, pltpu.roll(f, depth - 1, axis))
    before = jnp.where(z == 0, f, pltpu.roll(f, 1, axis))
    return after, before


def y_neighbours(f, low, high):
    count = f.shape[1]
    y = lax.broadcasted_iota(jnp.int32, f.shape, 1)
    after = jnp.where(y == count - 1, high[:, None, :], pltpu.roll(f, count - 1, 1))
    before = jnp.where(y == 0, low[:, None, :], pltpu.roll(f, 1, 1))
    return after, before


def x_neighbours(f, low, high):
    after = jnp.concatenate([f[1:], high[None]], 0)
    before = jnp.concatenate([low[None], f[:-1]], 0)
    return after, before


def gelu(x):
    c = math.sqrt(2.0 / math.pi)
    inner = x * (c + (c * 0.044715) * (x * x))
    h = 0.5 * x
    return h + h * jnp.tanh(inner)


def grouped(count, size, body):
    size = size if count % size == 0 else 1

    def go(g, carry):
        for s in range(size):
            body(g * size + s)
        return carry

    lax.fori_loop(0, count // size, go, 0)


def step_kernel(
    ngx, ngy,
    scal_hbm, vel_hbm, dif_hbm, list_hbm, win_hbm, wmid_hbm, wout_hbm,
    exy_hbm, ez_hbm, czh_hbm, czl_hbm, tyh_hbm, tyl_hbm, txh_hbm, txl_hbm,
    out, vout,
    scal, vel, dif, listed, w_in, w_mid, w_out, exy, ez, cz_h, cz_l, ty_h, ty_l, tx_h, tx_l,
    xsend, ysend, xrecv, yrecv,
    x2send, y2send, x2recv, y2recv,
    psx, psy, prx, pry, gsx, gsy, grx, gry,
    coef, section, asend, arecv, bsend, brecv, plane, modes, feeds, rates,
    in_sem, g_sem, h_sem, h2_sem, p_sem, a_sem, b_sem,
):
    channels, cx, cy, nz = scal.shape
    n = ngx * ngy
    kc = nz // n
    cells = cx * cy
    slots = listed.shape[1]
    f32, bf16 = jnp.float32, jnp.bfloat16
    i = lax.axis_index("gx")
    j = lax.axis_index("gy")
    me = i * ngy + j
    up_x = (lax.rem(i + 1, ngx), j)
    down_x = (lax.rem(i + ngx - 1, ngx), j)
    up_y = (i, lax.rem(j + 1, ngy))
    down_y = (i, lax.rem(j + ngy - 1, ngy))

    sources = (vel_hbm, dif_hbm, scal_hbm, list_hbm, czh_hbm, czl_hbm, ez_hbm.at[me], exy_hbm,
               tyh_hbm, tyl_hbm, txh_hbm, txl_hbm, win_hbm, wmid_hbm, wout_hbm)
    targets = (vel, dif, scal, listed, cz_h, cz_l, ez, exy,
               ty_h, ty_l, tx_h, tx_l, w_in, w_mid, w_out)
    fetches = [
        pltpu.make_async_copy(a, b, in_sem.at[at]) for at, (a, b) in enumerate(zip(sources, targets))
    ]
    for fetch in fetches[:3]:
        fetch.start()

    columns = [lax.rem(j + dj, ngy) for dj in range(ngy)]

    def others(fn):
        for dj in range(1, ngy):
            fn(i, columns[dj])

        def row(di, carry):
            i2 = lax.rem(i + di, ngx)
            for dj in range(ngy):
                fn(i2, columns[dj])
            return carry

        lax.fori_loop(1, ngx, row, 0)

    barrier = pltpu.get_barrier_semaphore()
    others(lambda i2, j2: pl.semaphore_signal(barrier, inc=1, device_id=(i2, j2), device_id_type=MESH))

    for fetch in fetches[:2]:
        fetch.wait()
    for side, at in ((0, cx - 1), (1, 0)):
        gsx[side, 0] = vel[0, at]
        gsx[side, 1] = dif[at]
    for side, at in ((0, cy - 1), (1, 0)):
        gsy[side, 0] = vel[1, :, at, :]
        gsy[side, 1] = dif[:, at, :]
    fetches[2].wait()

    def pack(c, f, xs, ys):
        xs[0, c] = f[cx - 1].astype(bf16)
        xs[1, c] = f[0].astype(bf16)
        ys[0, c] = f[:, cy - 1, :].astype(bf16)
        ys[1, c] = f[:, 0, :].astype(bf16)

    grouped(channels, 4, lambda c: pack(c, scal[c], xsend, ysend))
    pl.semaphore_wait(barrier, n - 1)

    def halo(xs, ys, xr, yr, sems):
        copies = []
        plan = ((xs, xr, 0, up_x), (xs, xr, 1, down_x), (ys, yr, 0, up_y), (ys, yr, 1, down_y))
        for at, (s, r, side, target) in enumerate(plan):
            copy = pltpu.make_async_remote_copy(
                src_ref=s.at[side], dst_ref=r.at[side], send_sem=sems.at[0, at],
                recv_sem=sems.at[1, at], device_id=target, device_id_type=MESH,
            )
            copy.start()
            copies.append(copy)
        return copies

    def everyone(send, recv, sems):
        def go(i2, j2):
            pltpu.make_async_remote_copy(
                src_ref=send.at[i2 * ngy + j2], dst_ref=recv.at[me], send_sem=sems.at[0],
                recv_sem=sems.at[1], device_id=(i2, j2), device_id_type=MESH,
            ).start()

        others(go)
        recv[me] = send[me]

    def everyone_wait(recv, sems, side):
        part = recv.at[pl.ds(0, n - 1)]
        pltpu.make_async_copy(part, part, sems.at[side]).wait()

    flow_halo = halo(gsx, gsy, grx, gry, g_sem)
    first_halo = halo(xsend, ysend, xrecv, yrecv, h_sem)
    for fetch in fetches[3:]:
        fetch.start()
    for fetch in fetches[3:6]:
        fetch.wait()
    cell = lax.broadcasted_iota(jnp.int32, (cells, slots), 0)
    put = (cell == listed[...]).astype(f32)
    take = put.T.astype(bf16)
    put = jnp.concatenate([put, put], 1).astype(bf16)
    for copy in flow_halo:
        copy.wait()

    u, v, w = vel[0], vel[1], vel[2]
    un, up = x_neighbours(u, grx[0, 0], grx[1, 0])
    vn, vp = y_neighbours(v, gry[0, 0], gry[1, 0])
    wn, wp = z_neighbours(w)
    div = 0.5 * (un - up) + 0.5 * (vn - vp) + 0.5 * (wn - wp)
    div = div.reshape(cells, nz)
    spec = dot3((cz_h[...], cz_l[...]), split(div), ((1,), (1,)))
    for d in range(n):
        asend[d] = spec[d * kc:(d + 1) * kc]
    everyone(asend, arecv, a_sem)

    k = dif[...]
    kxn, kxp = x_neighbours(k, grx[0, 1], grx[1, 1])
    kyn, kyp = y_neighbours(k, gry[0, 1], gry[1, 1])
    kzn, kzp = z_neighbours(k)
    half = 0.5 * time_step
    total = None
    for at, (nb, flow) in enumerate(((kxn, -u), (kxp, u), (kyn, -v), (kyp, v), (kzn, -w), (kzp, w))):
        face = k + nb
        coef[at] = half * (face + flow)
        total = face if total is None else total + face
    coef[6] = half * total

    def advance(f, c, xr, yr):
        xl, xh, yl, yh = (r[side, c].astype(f32) for r in (xr, yr) for side in (0, 1))
        xn, xp = x_neighbours(f, xl, xh)
        rate = coef[0] * xn + coef[1] * xp - coef[6] * f
        yn, yp = y_neighbours(f, yl, yh)
        rate = rate + (coef[2] * yn + coef[3] * yp)
        zn, zp = z_neighbours(f)
        return f + (rate + (coef[4] * zn + coef[5] * zp))

    for copy in first_halo:
        copy.wait()

    def first(c):
        s = advance(scal[c], c, xrecv, yrecv)
        section[c] = s
        pack(c, s, x2send, y2send)

    grouped(channels, 2, first)
    second_halo = halo(x2send, y2send, x2recv, y2recv, h2_sem)

    for fetch in fetches[6:]:
        fetch.wait()
    rows = ngx * kc
    ny = cy * ngy
    eigen = exy[...] + jnp.concatenate([ez[...]] * (cx * rows // ez.shape[0]), 0)
    minv = jnp.where(eigen == 0.0, 0.0, -1.0 / jnp.where(eigen == 0.0, 1.0, eigen))
    everyone_wait(arecv, a_sem, 1)
    for d in range(n):
        a, b = divmod(d, ngy)
        plane[a * kc:(a + 1) * kc, b * cells:(b + 1) * cells] = arecv[d]
    table_y = (ty_h[...], ty_l[...])
    table_x = (tx_h[...], tx_l[...])
    along = dot3(split(plane[...]), table_y)
    along = jnp.concatenate([along[:, a * ny:(a + 1) * ny] for a in range(cx)], 0)
    along = dot3(table_x, split(along)) * minv
    along = dot3(table_x, split(along))
    along = jnp.concatenate([along[a * rows:(a + 1) * rows] for a in range(cx)], 1)
    along = dot3(split(along), table_y, ((1,), (1,)))
    for d in range(n):
        a, b = divmod(d, ngy)
        bsend[d] = along[a * kc:(a + 1) * kc, b * cells:(b + 1) * cells]
    everyone(bsend, brecv, b_sem)

    for copy in second_halo:
        copy.wait()

    def second(c):
        s = advance(section[c], c, x2recv, y2recv)
        t = 0.5 * scal[c] + 0.5 * s
        out[c] = t
        feeds[pl.ds(c * slots, slots), :] = jnp.dot(
            take, t.reshape(cells, nz).astype(bf16), preferred_element_type=f32
        )

    grouped(channels, 2, second)

    def react(g, carry):
        base = g * BUNDLE
        feed = jnp.concatenate(
            [feeds[pl.ds(base + s, channels, stride=slots), :] for s in range(BUNDLE)], 1
        ).astype(bf16)
        one = lax.dot_general(w_in[...], feed, (((0,), (0,)), ((), ())), preferred_element_type=f32)
        one = gelu(one.astype(bf16))
        two = gelu(jnp.dot(w_mid[...], one, preferred_element_type=f32)).astype(bf16)
        rate = jnp.dot(w_out[...], two, preferred_element_type=f32)
        for s in range(BUNDLE):
            rates[pl.ds(base + s, channels, stride=slots), :] = rate[:, s * nz:(s + 1) * nz]
        return carry

    bundles = slots // BUNDLE
    cut_one, cut_two = bundles * 3 // 8, bundles * 6 // 8
    lax.fori_loop(0, cut_one, react, 0)

    everyone_wait(brecv, b_sem, 1)
    for d in range(n):
        modes[d * kc:(d + 1) * kc] = brecv[d]
    pressure = dot3(split(modes[...].T), (cz_h[...], cz_l[...])).reshape(cx, cy, nz)
    psx[0] = pressure[cx - 1]
    psx[1] = pressure[0]
    psy[0] = pressure[:, cy - 1, :]
    psy[1] = pressure[:, 0, :]
    last = halo(psx, psy, prx, pry, p_sem)
    zn, zp = z_neighbours(pressure)
    vout[2] = vel[2] - 0.5 * (zn - zp)
    section[0] = pressure

    lax.fori_loop(cut_one, cut_two, react, 0)

    for copy in last:
        copy.wait()
    pressure = section[0]
    xn, xp = x_neighbours(pressure, prx[0], prx[1])
    vout[0] = vel[0] - 0.5 * (xn - xp)
    yn, yp = y_neighbours(pressure, pry[0], pry[1])
    vout[1] = vel[1] - 0.5 * (yn - yp)

    lax.fori_loop(cut_two, bundles, react, 0)

    def scatter(c):
        parts = jnp.concatenate(split(rates[pl.ds(c * slots, slots), :]), 0)
        added = jnp.dot(put, parts, preferred_element_type=f32)
        out[c] = out[c] + added.reshape(cx, cy, nz)

    grouped(channels, 4, scatter)
    everyone_wait(arecv, a_sem, 0)
    everyone_wait(brecv, b_sem, 0)


def fast_shards(scalars, velocity, diffusivity, burn_list, w_in, w_mid, w_out):
    ngx, ngy = lax.axis_size("gx"), lax.axis_size("gy")
    channels, cx, cy, nz = scalars.shape
    n = ngx * ngy
    kc = nz // n
    nx, ny = cx * ngx, cy * ngy
    hx, hy = hartley_np(nx), hartley_np(ny)
    ty = np.einsum("ab,cjy->jaybc", np.eye(cx), hy.reshape(ny, ngy, cy)).reshape(ngy * cx * cy, cx * ny)
    order = (np.arange(ngx)[None, :] * cx + np.arange(cx)[:, None]).reshape(-1)
    tx = np.kron(hx[np.ix_(order, order)], np.eye(kc))
    ex = np.repeat(2.0 - 2.0 * np.cos(2.0 * np.pi / nx * order), kc)
    ey = 2.0 - 2.0 * np.cos(2.0 * np.pi / ny * np.arange(ny))
    exy = (ex[:, None] + ey[None, :]).astype(np.float32)
    ez = 2.0 - 2.0 * np.cos(np.pi / nz * np.arange(nz))
    ez = np.tile(ez.reshape(n, kc, 1), (1, max(1, 8 // kc), ny)).astype(np.float32)
    tables = [t for pair in (split_np(cosine_np(nz)), split_np(ty), split_np(tx)) for t in pair]
    operands = [
        scalars, velocity, diffusivity, burn_list.reshape(1, -1), w_in.T, w_mid, w_out,
        *(jnp.asarray(t) for t in (exy, ez, *tables)),
    ]
    f32 = jnp.float32
    slots = operands[3].shape[1]
    vm = pl.BlockSpec(memory_space=pltpu.VMEM)
    copies = [pltpu.VMEM(a.shape, a.dtype) for a in operands]
    copies[8] = pltpu.VMEM(ez.shape[1:], f32)
    halo_scratch = lambda c, t: [pltpu.VMEM((2, c, cy, nz), t), pltpu.VMEM((2, c, cx, nz), t)]
    face_scratch = [pltpu.VMEM((2, cy, nz), f32), pltpu.VMEM((2, cx, nz), f32)]
    chunk = pltpu.VMEM((n, kc, cx * cy), f32)
    dma = pltpu.SemaphoreType.DMA
    return pl.pallas_call(
        functools.partial(step_kernel, ngx, ngy),
        out_shape=(jax.ShapeDtypeStruct(scalars.shape, f32), jax.ShapeDtypeStruct(velocity.shape, f32)),
        in_specs=[pl.BlockSpec(memory_space=pl.ANY)] * len(operands),
        out_specs=(vm, vm),
        scratch_shapes=copies + halo_scratch(channels, jnp.bfloat16) * 4 + face_scratch * 2 + halo_scratch(2, f32) * 2 + [
            pltpu.VMEM((7, cx, cy, nz), f32), pltpu.VMEM(scalars.shape, f32),
            chunk, chunk, chunk, chunk,
            pltpu.VMEM((ngx * kc, ngy * cx * cy), f32), pltpu.VMEM((nz, cx * cy), f32),
            pltpu.VMEM((channels * slots, nz), f32), pltpu.VMEM((channels * slots, nz), f32),
            dma((len(operands),)), dma((2, 4)), dma((2, 4)), dma((2, 4)), dma((2, 4)), dma((2,)), dma((2,)),
        ],
        compiler_params=pltpu.CompilerParams(
            collective_id=0, has_side_effects=True, vmem_limit_bytes=60 * 1024 * 1024
        ),
    )(*operands)


def local_shards(scalars, velocity, diffusivity, *rest):
    depth = scalars.shape[-1]
    devices = lax.axis_size("gx") * lax.axis_size("gy")
    whole_chunks = depth % devices == 0 and 8 % (depth // devices) == 0
    plan = fast_shards if whole_chunks else shards
    return plan(scalars, velocity, diffusivity, *rest)


def solution(mesh):
    in_specs = (
        P(None, "gx", "gy", None),
        P(None, "gx", "gy", None),
        P("gx", "gy", None),
        P("gx", "gy", None),
        P(),
        P(),
        P(),
    )
    out_specs = (P(None, "gx", "gy", None), P(None, "gx", "gy", None))
    return jax.shard_map(local_shards, mesh=mesh, in_specs=in_specs, out_specs=out_specs, check_vma=False)
```

```python
import functools
import math

import jax
import jax.numpy as jnp
import numpy as np
from jax import lax
from jax.experimental import pallas as pl
from jax.experimental.pallas import tpu as pltpu
from jax.sharding import PartitionSpec as P

time_step = 0.25


def with_halo(block, sides, width):
    for axis, dim in sides:
        count = lax.axis_size(axis)
        forward = [(i, i + 1) for i in range(count - 1)]
        forward.append((count - 1, 0))
        backward = [(target, source) for source, target in forward]
        low = lax.ppermute(
            lax.slice_in_dim(block, block.shape[dim] - width, None, axis=dim), axis, forward
        )
        high = lax.ppermute(lax.slice_in_dim(block, 0, width, axis=dim), axis, backward)
        block = jnp.concatenate([low, block, high], axis=dim)
    return block


def hartley_table(length):
    position = jnp.arange(length, dtype=jnp.int32)
    product = position[:, None] * position[None, :] % length
    phase_angle = 2.0 * math.pi / length * product.astype(jnp.float32)
    return (jnp.cos(phase_angle) + jnp.sin(phase_angle)) / math.sqrt(length)


def cosine_table(length):
    position = jnp.arange(length, dtype=jnp.int32)
    product = position[:, None] * (2 * position[None, :] + 1) % (4 * length)
    phase_angle = math.pi / (2 * length) * product.astype(jnp.float32)
    weight = jnp.where(position == 0, math.sqrt(1.0 / length), math.sqrt(2.0 / length)).astype(
        jnp.float32
    )
    return weight[:, None] * jnp.cos(phase_angle)


def depth_next(values):
    return jnp.concatenate([values[..., 1:], values[..., -1:]], -1)


def depth_prev(values):
    return jnp.concatenate([values[..., :1], values[..., :-1]], -1)


def transport_rate(field_pad, flow_pad):
    center = field_pad[:, 1:-1, 1:-1]
    x_next = field_pad[:, 2:, 1:-1]
    x_prev = field_pad[:, :-2, 1:-1]
    y_next = field_pad[:, 1:-1, 2:]
    y_prev = field_pad[:, 1:-1, :-2]
    z_next = depth_next(center)
    z_prev = depth_prev(center)
    coefficient = flow_pad[3, 1:-1, 1:-1]
    advection = (
        flow_pad[0, 1:-1, 1:-1] * (x_next - x_prev) * 0.5
        + flow_pad[1, 1:-1, 1:-1] * (y_next - y_prev) * 0.5
        + flow_pad[2, 1:-1, 1:-1] * (z_next - z_prev) * 0.5
    )
    diffusion = 0.5 * (coefficient + flow_pad[3, 2:, 1:-1]) * (x_next - center) - 0.5 * (
        coefficient + flow_pad[3, :-2, 1:-1]
    ) * (center - x_prev)
    diffusion = (
        diffusion
        + 0.5 * (coefficient + flow_pad[3, 1:-1, 2:]) * (y_next - center)
        - 0.5 * (coefficient + flow_pad[3, 1:-1, :-2]) * (center - y_prev)
    )
    diffusion = (
        diffusion
        + 0.5 * (coefficient + depth_next(coefficient)) * (z_next - center)
        - 0.5 * (coefficient + depth_prev(coefficient)) * (center - z_prev)
    )
    return diffusion - advection


def network(blocks, w_in, w_mid, w_out):
    block_count = blocks.shape[0]
    bundle_size = 8
    padded_count = -(-block_count // bundle_size) * bundle_size

    def evaluate(bundle):
        hidden_one = jnp.einsum("hn,bnz->bhz", w_in, bundle, preferred_element_type=jnp.float32)
        hidden_one = jax.nn.gelu(hidden_one).astype(jnp.bfloat16)
        hidden_two = jnp.einsum(
            "kh,bhz->bkz", w_mid, hidden_one, preferred_element_type=jnp.float32
        )
        hidden_two = jax.nn.gelu(hidden_two).astype(jnp.bfloat16)
        return jnp.einsum("nk,bkz->bnz", w_out, hidden_two, preferred_element_type=jnp.float32)

    reaction = lax.map(
        evaluate, blocks.reshape((padded_count // bundle_size, bundle_size) + blocks.shape[1:])
    )
    return reaction.reshape((padded_count,) + reaction.shape[2:])


def solve_modes(spectrum, start_y, start_z, total_x, total_y, total_z):
    mode_x = jnp.arange(spectrum.shape[0], dtype=jnp.int32)
    mode_y = start_y + jnp.arange(spectrum.shape[1], dtype=jnp.int32)
    mode_z = start_z + jnp.arange(spectrum.shape[2], dtype=jnp.int32)
    eigen_x = 2.0 - 2.0 * jnp.cos(2.0 * math.pi / total_x * mode_x.astype(jnp.float32))
    eigen_y = 2.0 - 2.0 * jnp.cos(2.0 * math.pi / total_y * mode_y.astype(jnp.float32))
    eigen_z = 2.0 - 2.0 * jnp.cos(math.pi / total_z * mode_z.astype(jnp.float32))
    eigen = eigen_x[:, None, None] + eigen_y[None, :, None] + eigen_z[None, None, :]
    anchor = (
        (mode_x[:, None, None] == 0) & (mode_y[None, :, None] == 0) & (mode_z[None, None, :] == 0)
    ).astype(jnp.float32)
    return -spectrum * (1.0 - anchor) / (eigen + anchor)


def shards(scalars, velocity, diffusivity, burn_list, w_in, w_mid, w_out):
    channels = scalars.shape[0]
    joined = jnp.concatenate([scalars, velocity, diffusivity[None]], 0)
    padded = with_halo(joined, (("gx", 1), ("gy", 2)), 1)
    field_pad = padded[:channels]
    inner_flow = padded[channels:]
    section_one = scalars + time_step * transport_rate(field_pad, inner_flow)
    section_pad = with_halo(section_one, (("gx", 1), ("gy", 2)), 1)
    transported = 0.5 * scalars + 0.5 * (
        section_one + time_step * transport_rate(section_pad, inner_flow)
    )
    divergence = 0.5 * (inner_flow[0, 2:, 1:-1] - inner_flow[0, :-2, 1:-1])
    divergence = divergence + 0.5 * (inner_flow[1, 1:-1, 2:] - inner_flow[1, 1:-1, :-2])
    vertical = inner_flow[2, 1:-1, 1:-1]
    divergence = divergence + 0.5 * (depth_next(vertical) - depth_prev(vertical))
    highest = lax.Precision.HIGHEST
    cells_x, cells_y, depth = divergence.shape
    total_x = cells_x * lax.axis_size("gx")
    total_y = cells_y * lax.axis_size("gy")
    table_x = hartley_table(total_x)
    table_y = hartley_table(total_y)
    table_z = cosine_table(depth)
    spectrum = jnp.einsum("az,xyz->xya", table_z, divergence, precision=highest)
    along_y = lax.all_to_all(spectrum, "gy", split_axis=2, concat_axis=1, tiled=True)
    along_y = jnp.einsum("by,xyz->xbz", table_y, along_y, precision=highest)
    along_x = lax.all_to_all(
        along_y.astype(jnp.bfloat16), "gx", split_axis=1, concat_axis=0, tiled=True
    ).astype(along_y.dtype)
    along_x = jnp.einsum("cx,xyz->cyz", table_x, along_x, precision=highest)
    solved = solve_modes(
        along_x,
        lax.axis_index("gx") * along_x.shape[1],
        lax.axis_index("gy") * along_x.shape[2],
        total_x,
        total_y,
        depth,
    )
    solved = jnp.einsum("cx,xyz->cyz", table_x, solved, precision=highest)
    solved = lax.all_to_all(solved, "gx", split_axis=0, concat_axis=1, tiled=True)
    solved = jnp.einsum("by,xyz->xbz", table_y, solved, precision=highest)
    solved = lax.all_to_all(solved, "gy", split_axis=1, concat_axis=2, tiled=True)
    pressure = jnp.einsum("az,xya->xyz", table_z, solved, precision=highest)
    pressure_pad = with_halo(pressure, (("gx", 0), ("gy", 1)), 1)
    grad_x = 0.5 * (pressure_pad[2:, 1:-1] - pressure_pad[:-2, 1:-1])
    grad_y = 0.5 * (pressure_pad[1:-1, 2:] - pressure_pad[1:-1, :-2])
    grad_z = 0.5 * (depth_next(pressure) - depth_prev(pressure))
    velocity_out = velocity - jnp.stack([grad_x, grad_y, grad_z])
    block_total = cells_x * cells_y
    flat_blocks = transported.reshape(channels, block_total, depth)
    listed = burn_list.reshape(-1)
    picked = jnp.take(flat_blocks, jnp.minimum(listed, block_total - 1), axis=1)
    chosen = jnp.transpose(picked, (1, 0, 2)).astype(jnp.bfloat16)
    own_rates = network(chosen, w_in, w_mid, w_out)
    updated = flat_blocks.at[:, listed].add(jnp.transpose(own_rates, (1, 0, 2)), mode="drop")
    scalars_out = updated.reshape(transported.shape)
    return (scalars_out, velocity_out)


MESH = pl.DeviceIdType.MESH
BUNDLE = 8


def hartley_np(length):
    product = np.outer(np.arange(length), np.arange(length)) % length
    angle = 2.0 * np.pi / length * product
    return (np.cos(angle) + np.sin(angle)) / np.sqrt(length)


def cosine_np(length):
    k = np.arange(length)
    angle = np.pi / (2 * length) * (np.outer(k, 2 * k + 1) % (4 * length))
    weight = np.where(k == 0, np.sqrt(1.0 / length), np.sqrt(2.0 / length))
    return weight[:, None] * np.cos(angle)


def split_np(table):
    high = table.astype(jnp.bfloat16)
    low = (table - high.astype(np.float64)).astype(jnp.bfloat16)
    return high, low


def split(value):
    high = value.astype(jnp.bfloat16)
    return high, (value - high.astype(jnp.float32)).astype(jnp.bfloat16)


def dot3(a, b, dims=((1,), (0,))):
    run = lambda p, q: lax.dot_general(p, q, (dims, ((), ())), preferred_element_type=jnp.float32)
    return run(a[0], b[0]) + (run(a[1], b[0]) + run(a[0], b[1]))


def z_neighbours(f):
    axis = f.ndim - 1
    depth = f.shape[axis]
    z = lax.broadcasted_iota(jnp.int32, f.shape, axis)
    after = jnp.where(z == depth - 1, f, pltpu.roll(f, depth - 1, axis))
    before = jnp.where(z == 0, f, pltpu.roll(f, 1, axis))
    return after, before


def y_neighbours(f, low, high):
    count = f.shape[1]
    y = lax.broadcasted_iota(jnp.int32, f.shape, 1)
    after = jnp.where(y == count - 1, high[:, None, :], pltpu.roll(f, count - 1, 1))
    before = jnp.where(y == 0, low[:, None, :], pltpu.roll(f, 1, 1))
    return after, before


def x_neighbours(f, low, high):
    after = jnp.concatenate([f[1:], high[None]], 0)
    before = jnp.concatenate([low[None], f[:-1]], 0)
    return after, before


def gelu(x):
    c = math.sqrt(2.0 / math.pi)
    inner = x * (c + (c * 0.044715) * (x * x))
    h = 0.5 * x
    return h + h * jnp.tanh(inner)


def grouped(count, size, body):
    size = size if count % size == 0 else 1

    def go(g, carry):
        for s in range(size):
            body(g * size + s)
        return carry

    lax.fori_loop(0, count // size, go, 0)


def step_kernel(
    ngx, ngy,
    scal_hbm, vel_hbm, dif_hbm, list_hbm, win_hbm, wmid_hbm, wout_hbm,
    exy_hbm, ez_hbm, czh_hbm, czl_hbm, tyh_hbm, tyl_hbm, txh_hbm, txl_hbm,
    out, vout,
    scal, vel, dif, listed, w_in, w_mid, w_out, exy, ez, cz_h, cz_l, ty_h, ty_l, tx_h, tx_l,
    xsend, ysend, xrecv, yrecv,
    x2send, y2send, x2recv, y2recv,
    psx, psy, prx, pry, gsx, gsy, grx, gry,
    coef, section, asend, arecv, bsend, brecv, plane, modes, feeds, rates,
    in_sem, g_sem, h_sem, h2_sem, p_sem, a_sem, b_sem,
):
    channels, cx, cy, nz = scal.shape
    n = ngx * ngy
    kc = nz // n
    cells = cx * cy
    slots = listed.shape[1]
    f32, bf16 = jnp.float32, jnp.bfloat16
    i = lax.axis_index("gx")
    j = lax.axis_index("gy")
    me = i * ngy + j
    up_x = (lax.rem(i + 1, ngx), j)
    down_x = (lax.rem(i + ngx - 1, ngx), j)
    up_y = (i, lax.rem(j + 1, ngy))
    down_y = (i, lax.rem(j + ngy - 1, ngy))

    sources = (vel_hbm, dif_hbm, scal_hbm, list_hbm, czh_hbm, czl_hbm, ez_hbm.at[me], exy_hbm,
               tyh_hbm, tyl_hbm, txh_hbm, txl_hbm, win_hbm, wmid_hbm, wout_hbm)
    targets = (vel, dif, scal, listed, cz_h, cz_l, ez, exy,
               ty_h, ty_l, tx_h, tx_l, w_in, w_mid, w_out)
    fetches = [
        pltpu.make_async_copy(a, b, in_sem.at[at]) for at, (a, b) in enumerate(zip(sources, targets))
    ]
    for fetch in fetches[:3]:
        fetch.start()

    columns = [lax.rem(j + dj, ngy) for dj in range(ngy)]

    def others(fn):
        for dj in range(1, ngy):
            fn(i, columns[dj])

        def row(di, carry):
            i2 = lax.rem(i + di, ngx)
            for dj in range(ngy):
                fn(i2, columns[dj])
            return carry

        lax.fori_loop(1, ngx, row, 0)

    barrier = pltpu.get_barrier_semaphore()
    others(lambda i2, j2: pl.semaphore_signal(barrier, inc=1, device_id=(i2, j2), device_id_type=MESH))

    for fetch in fetches[:2]:
        fetch.wait()
    for side, at in ((0, cx - 1), (1, 0)):
        gsx[side, 0] = vel[0, at]
        gsx[side, 1] = dif[at]
    for side, at in ((0, cy - 1), (1, 0)):
        gsy[side, 0] = vel[1, :, at, :]
        gsy[side, 1] = dif[:, at, :]
    fetches[2].wait()

    def pack(c, f, xs, ys):
        xs[0, c] = f[cx - 1].astype(bf16)
        xs[1, c] = f[0].astype(bf16)
        ys[0, c] = f[:, cy - 1, :].astype(bf16)
        ys[1, c] = f[:, 0, :].astype(bf16)

    grouped(channels, 4, lambda c: pack(c, scal[c], xsend, ysend))
    pl.semaphore_wait(barrier, n - 1)

    def halo(xs, ys, xr, yr, sems):
        copies = []
        plan = ((xs, xr, 0, up_x), (xs, xr, 1, down_x), (ys, yr, 0, up_y), (ys, yr, 1, down_y))
        for at, (s, r, side, target) in enumerate(plan):
            copy = pltpu.make_async_remote_copy(
                src_ref=s.at[side], dst_ref=r.at[side], send_sem=sems.at[0, at],
                recv_sem=sems.at[1, at], device_id=target, device_id_type=MESH,
            )
            copy.start()
            copies.append(copy)
        return copies

    def everyone(send, recv, sems):
        def go(i2, j2):
            pltpu.make_async_remote_copy(
                src_ref=send.at[i2 * ngy + j2], dst_ref=recv.at[me], send_sem=sems.at[0],
                recv_sem=sems.at[1], device_id=(i2, j2), device_id_type=MESH,
            ).start()

        others(go)
        recv[me] = send[me]

    def everyone_wait(recv, sems, side):
        part = recv.at[pl.ds(0, n - 1)]
        pltpu.make_async_copy(part, part, sems.at[side]).wait()

    flow_halo = halo(gsx, gsy, grx, gry, g_sem)
    first_halo = halo(xsend, ysend, xrecv, yrecv, h_sem)
    for fetch in fetches[3:]:
        fetch.start()
    for fetch in fetches[3:6]:
        fetch.wait()
    cell = lax.broadcasted_iota(jnp.int32, (cells, slots), 0)
    put = (cell == listed[...]).astype(f32)
    take = put.T.astype(bf16)
    put = jnp.concatenate([put, put], 1).astype(bf16)
    for copy in flow_halo:
        copy.wait()

    u, v, w = vel[0], vel[1], vel[2]
    un, up = x_neighbours(u, grx[0, 0], grx[1, 0])
    vn, vp = y_neighbours(v, gry[0, 0], gry[1, 0])
    wn, wp = z_neighbours(w)
    div = 0.5 * (un - up) + 0.5 * (vn - vp) + 0.5 * (wn - wp)
    div = div.reshape(cells, nz)
    spec = dot3((cz_h[...], cz_l[...]), split(div), ((1,), (1,)))
    for d in range(n):
        asend[d] = spec[d * kc:(d + 1) * kc]
    everyone(asend, arecv, a_sem)

    k = dif[...]
    kxn, kxp = x_neighbours(k, grx[0, 1], grx[1, 1])
    kyn, kyp = y_neighbours(k, gry[0, 1], gry[1, 1])
    kzn, kzp = z_neighbours(k)
    half = 0.5 * time_step
    total = None
    for at, (nb, flow) in enumerate(((kxn, -u), (kxp, u), (kyn, -v), (kyp, v), (kzn, -w), (kzp, w))):
        face = k + nb
        coef[at] = half * (face + flow)
        total = face if total is None else total + face
    coef[6] = half * total

    def advance(f, c, xr, yr):
        xl, xh, yl, yh = (r[side, c].astype(f32) for r in (xr, yr) for side in (0, 1))
        xn, xp = x_neighbours(f, xl, xh)
        rate = coef[0] * xn + coef[1] * xp - coef[6] * f
        yn, yp = y_neighbours(f, yl, yh)
        rate = rate + (coef[2] * yn + coef[3] * yp)
        zn, zp = z_neighbours(f)
        return f + (rate + (coef[4] * zn + coef[5] * zp))

    for copy in first_halo:
        copy.wait()

    def first(c):
        s = advance(scal[c], c, xrecv, yrecv)
        section[c] = s
        pack(c, s, x2send, y2send)

    grouped(channels, 2, first)
    second_halo = halo(x2send, y2send, x2recv, y2recv, h2_sem)

    for fetch in fetches[6:]:
        fetch.wait()
    rows = ngx * kc
    ny = cy * ngy
    eigen = exy[...] + jnp.concatenate([ez[...]] * (cx * rows // ez.shape[0]), 0)
    minv = jnp.where(eigen == 0.0, 0.0, -1.0 / jnp.where(eigen == 0.0, 1.0, eigen))
    everyone_wait(arecv, a_sem, 1)
    for d in range(n):
        a, b = divmod(d, ngy)
        plane[a * kc:(a + 1) * kc, b * cells:(b + 1) * cells] = arecv[d]
    table_y = (ty_h[...], ty_l[...])
    table_x = (tx_h[...], tx_l[...])
    along = dot3(split(plane[...]), table_y)
    along = jnp.concatenate([along[:, a * ny:(a + 1) * ny] for a in range(cx)], 0)
    along = dot3(table_x, split(along)) * minv
    along = dot3(table_x, split(along))
    along = jnp.concatenate([along[a * rows:(a + 1) * rows] for a in range(cx)], 1)
    along = dot3(split(along), table_y, ((1,), (1,)))
    for d in range(n):
        a, b = divmod(d, ngy)
        bsend[d] = along[a * kc:(a + 1) * kc, b * cells:(b + 1) * cells]
    everyone(bsend, brecv, b_sem)

    for copy in second_halo:
        copy.wait()

    def second(c):
        s = advance(section[c], c, x2recv, y2recv)
        t = 0.5 * scal[c] + 0.5 * s
        out[c] = t
        feeds[pl.ds(c * slots, slots), :] = jnp.dot(
            take, t.reshape(cells, nz).astype(bf16), preferred_element_type=f32
        )

    grouped(channels, 2, second)

    def react(g, carry):
        base = g * BUNDLE
        feed = jnp.concatenate(
            [feeds[pl.ds(base + s, channels, stride=slots), :] for s in range(BUNDLE)], 1
        ).astype(bf16)
        one = lax.dot_general(w_in[...], feed, (((0,), (0,)), ((), ())), preferred_element_type=f32)
        one = gelu(one.astype(bf16))
        two = gelu(jnp.dot(w_mid[...], one, preferred_element_type=f32).astype(bf16))
        rate = jnp.dot(w_out[...], two, preferred_element_type=f32)
        for s in range(BUNDLE):
            rates[pl.ds(base + s, channels, stride=slots), :] = rate[:, s * nz:(s + 1) * nz]
        return carry

    bundles = slots // BUNDLE
    cut_one, cut_two = bundles * 3 // 8, bundles * 6 // 8
    lax.fori_loop(0, cut_one, react, 0)

    everyone_wait(brecv, b_sem, 1)
    for d in range(n):
        modes[d * kc:(d + 1) * kc] = brecv[d]
    pressure = dot3(split(modes[...].T), (cz_h[...], cz_l[...])).reshape(cx, cy, nz)
    psx[0] = pressure[cx - 1]
    psx[1] = pressure[0]
    psy[0] = pressure[:, cy - 1, :]
    psy[1] = pressure[:, 0, :]
    last = halo(psx, psy, prx, pry, p_sem)
    zn, zp = z_neighbours(pressure)
    vout[2] = vel[2] - 0.5 * (zn - zp)
    section[0] = pressure

    lax.fori_loop(cut_one, cut_two, react, 0)

    for copy in last:
        copy.wait()
    pressure = section[0]
    xn, xp = x_neighbours(pressure, prx[0], prx[1])
    vout[0] = vel[0] - 0.5 * (xn - xp)
    yn, yp = y_neighbours(pressure, pry[0], pry[1])
    vout[1] = vel[1] - 0.5 * (yn - yp)

    lax.fori_loop(cut_two, bundles, react, 0)

    def scatter(c):
        parts = jnp.concatenate(split(rates[pl.ds(c * slots, slots), :]), 0)
        added = jnp.dot(put, parts, preferred_element_type=f32)
        out[c] = out[c] + added.reshape(cx, cy, nz)

    grouped(channels, 4, scatter)
    everyone_wait(arecv, a_sem, 0)
    everyone_wait(brecv, b_sem, 0)


def fast_shards(scalars, velocity, diffusivity, burn_list, w_in, w_mid, w_out):
    ngx, ngy = lax.axis_size("gx"), lax.axis_size("gy")
    channels, cx, cy, nz = scalars.shape
    n = ngx * ngy
    kc = nz // n
    nx, ny = cx * ngx, cy * ngy
    hx, hy = hartley_np(nx), hartley_np(ny)
    ty = np.einsum("ab,cjy->jaybc", np.eye(cx), hy.reshape(ny, ngy, cy)).reshape(ngy * cx * cy, cx * ny)
    order = (np.arange(ngx)[None, :] * cx + np.arange(cx)[:, None]).reshape(-1)
    tx = np.kron(hx[np.ix_(order, order)], np.eye(kc))
    ex = np.repeat(2.0 - 2.0 * np.cos(2.0 * np.pi / nx * order), kc)
    ey = 2.0 - 2.0 * np.cos(2.0 * np.pi / ny * np.arange(ny))
    exy = (ex[:, None] + ey[None, :]).astype(np.float32)
    ez = 2.0 - 2.0 * np.cos(np.pi / nz * np.arange(nz))
    ez = np.tile(ez.reshape(n, kc, 1), (1, max(1, 8 // kc), ny)).astype(np.float32)
    tables = [t for pair in (split_np(cosine_np(nz)), split_np(ty), split_np(tx)) for t in pair]
    operands = [
        scalars, velocity, diffusivity, burn_list.reshape(1, -1), w_in.T, w_mid, w_out,
        *(jnp.asarray(t) for t in (exy, ez, *tables)),
    ]
    f32 = jnp.float32
    slots = operands[3].shape[1]
    vm = pl.BlockSpec(memory_space=pltpu.VMEM)
    copies = [pltpu.VMEM(a.shape, a.dtype) for a in operands]
    copies[8] = pltpu.VMEM(ez.shape[1:], f32)
    halo_scratch = lambda c, t: [pltpu.VMEM((2, c, cy, nz), t), pltpu.VMEM((2, c, cx, nz), t)]
    face_scratch = [pltpu.VMEM((2, cy, nz), f32), pltpu.VMEM((2, cx, nz), f32)]
    chunk = pltpu.VMEM((n, kc, cx * cy), f32)
    dma = pltpu.SemaphoreType.DMA
    return pl.pallas_call(
        functools.partial(step_kernel, ngx, ngy),
        out_shape=(jax.ShapeDtypeStruct(scalars.shape, f32), jax.ShapeDtypeStruct(velocity.shape, f32)),
        in_specs=[pl.BlockSpec(memory_space=pl.ANY)] * len(operands),
        out_specs=(vm, vm),
        scratch_shapes=copies + halo_scratch(channels, jnp.bfloat16) * 4 + face_scratch * 2 + halo_scratch(2, f32) * 2 + [
            pltpu.VMEM((7, cx, cy, nz), f32), pltpu.VMEM(scalars.shape, f32),
            chunk, chunk, chunk, chunk,
            pltpu.VMEM((ngx * kc, ngy * cx * cy), f32), pltpu.VMEM((nz, cx * cy), f32),
            pltpu.VMEM((channels * slots, nz), f32), pltpu.VMEM((channels * slots, nz), f32),
            dma((len(operands),)), dma((2, 4)), dma((2, 4)), dma((2, 4)), dma((2, 4)), dma((2,)), dma((2,)),
        ],
        compiler_params=pltpu.CompilerParams(
            collective_id=0, has_side_effects=True, vmem_limit_bytes=60 * 1024 * 1024
        ),
    )(*operands)


def local_shards(scalars, velocity, diffusivity, *rest):
    depth = scalars.shape[-1]
    devices = lax.axis_size("gx") * lax.axis_size("gy")
    whole_chunks = depth % devices == 0 and 8 % (depth // devices) == 0
    plan = fast_shards if whole_chunks else shards
    return plan(scalars, velocity, diffusivity, *rest)


def solution(mesh):
    in_specs = (
        P(None, "gx", "gy", None),
        P(None, "gx", "gy", None),
        P("gx", "gy", None),
        P("gx", "gy", None),
        P(),
        P(),
        P(),
    )
    out_specs = (P(None, "gx", "gy", None), P(None, "gx", "gy", None))
    return jax.shard_map(local_shards, mesh=mesh, in_specs=in_specs, out_specs=out_specs, check_vma=False)
```
